128 devices in a mesh: wide: 16 (over z_hi, y, core), narrow: 8 (over x, z_lo).
Axes of the slice: x: 4, y: 4, z: 4 (z_hi: 2, z_lo: 2; z = z_hi * 2 + z_lo), core: 2. Of those that a mesh axis runs over, the one named last changes fastest.
Arguments:
- field: float32 [4, 512, 512, 256], P(None, 'wide', 'narrow'), may hold values from -70 to 70, as said below
- start_first: float32 [512, 128], replicated, may hold values from -5 to 5
- start_second: float32 [512, 128], replicated, may hold values from -5 to 5
Outputs:
- core_tensor: float32 [256, 4, 128, 128], P('wide', None, 'narrow')
- basis_first: float32 [512, 128], replicated
- basis_second: float32 [512, 128], replicated
The draws below stay inside these ranges and needn't reach their ends.
Inputs may be any that keep to these rules, and one draw needn't show every extreme that they name: `field`: species fields with amplitudes that vary over mode 1, mode 2 and mode 3.
All inputs are finite; a program needn't handle non-finite values.
Results may differ from the reference program's by a relative error of at most 0.0003.
Values sent between devices are 32-bit elements; how exact they have to be, the bound alone decides.
No kernel may reach another device: no remote copies, remote signals or barrier semaphores. Data moves between devices by JAX's collectives and lax.ppermute only.
A program may use at most 192 MiB of HBM per device.

```python
import math
import jax
import jax.numpy as jnp
from jax import lax

I1 = 512
I2 = 512
S = 4
R1 = 128
R2 = 128
ITERS = 3
I3 = 256


def profile(key_rate, key_offset, position, count):
    frequency = jax.random.uniform(key_rate, (count,), jnp.float32, 0.5, 2.0)
    phases = jax.random.uniform(key_offset, (count,), jnp.float32, 0.0, 2.0 * math.pi)
    angle_grid = 2.0 * math.pi * (position[:, None] * frequency[None, :] + phases[None, :])
    return jnp.exp(math.log(10.0) * 0.5 * (1.0 + jnp.sin(angle_grid)))


def draw_field(key, part):
    subkeys = jax.random.split(jax.random.fold_in(key, 17), 6)
    full_shape = (S, I1, I2, I3)
    jitter = jnp.clip(jax.random.normal(subkeys[0], full_shape, jnp.float32), -4.0, 4.0)
    position = jnp.arange(I3, dtype=jnp.float32) / I3
    along_first = profile(subkeys[1], subkeys[2], position, I1)
    along_second = profile(subkeys[3], subkeys[4], position, I2)
    growth = jnp.sqrt(1.0 + 2.0 * position)
    species_scale = jnp.exp(jax.random.uniform(subkeys[5], (S,), jnp.float32, 0.0, math.log(3.0)))
    scaled = jitter * along_first.T[None, :, None, :] * along_second.T[None, None, :, :]
    scaled = scaled * growth[None, None, None, :] * species_scale[:, None, None, None]
    return scaled / 30.0


def noise(key, shape, scale, bound, kind=jnp.bfloat16):
    values = scale * jax.random.normal(key, shape, jnp.float32)
    return jnp.clip(values, min=-bound, max=bound).astype(kind)


def setup_inputs(seed: int = 0) -> dict:
    keys = jax.random.split(jax.random.key(seed), 4)
    return {
        "field": draw_field(jax.random.fold_in(keys[3], 71), 0),
        "start_first": noise(keys[1], (I1, R1), 1.0, 5.0, jnp.float32),
        "start_second": noise(keys[2], (I2, R2), 1.0, 5.0, jnp.float32),
    }


def orthonormal(columns):
    gram_matrix = jnp.dot(columns.T, columns, precision=lax.Precision.HIGHEST)
    lower_factor = jnp.linalg.cholesky(gram_matrix)
    return jax.scipy.linalg.solve_triangular(lower_factor, columns.T, lower=True).T

def iterate_basis(upper, start):
    basis_now = orthonormal(start)
    for sweep in range(ITERS):
        inner = jnp.dot(upper, basis_now, precision=lax.Precision.HIGHEST)
        basis_now = orthonormal(jnp.dot(upper.T, inner, precision=lax.Precision.HIGHEST))
    return basis_now

def reference(field, start_first, start_second):
    gram_first = jnp.einsum('sipt,sjpt->ij', field, field, precision=lax.Precision.HIGHEST)
    factor_first = jnp.linalg.cholesky(gram_first).T
    basis_first = iterate_basis(factor_first, start_first)
    reduced = jnp.einsum('ir,sipt->srpt', basis_first, field, precision=lax.Precision.HIGHEST)
    gram_second = jnp.einsum('srpt,srqt->pq', reduced, reduced, precision=lax.Precision.HIGHEST)
    factor_second = jnp.linalg.cholesky(gram_second).T
    basis_second = iterate_basis(factor_second, start_second)
    core_tensor = jnp.einsum('pq,srpt->tsrq', basis_second, reduced, precision=lax.Precision.HIGHEST)
    return (core_tensor, basis_first, basis_second)
```

```python
import functools
import jax
import jax.numpy as jnp
from jax import lax
from jax.experimental import pallas as pl
from jax.experimental.pallas import tpu as pltpu
from jax.sharding import PartitionSpec as P

ITERS = 3
F32 = jnp.float32
BF16 = jnp.bfloat16
EXACT = lax.Precision.HIGHEST
ALL = ("wide", "narrow")
VMEM_LIMIT = 60 * 1024 * 1024

NN = (((1,), (0,)), ((), ()))
NT = (((1,), (1,)), ((), ()))
TN = (((0,), (0,)), ((), ()))


def dot32(a, b, dims):
    return lax.dot_general(a, b, dims, precision=EXACT, preferred_element_type=F32)


def dot16(a, b, dims):
    return lax.dot_general(a, b, dims, preferred_element_type=F32)


def split2(x):
    high = x.astype(BF16)
    low = (x - high.astype(F32)).astype(BF16)
    return high, low


def split3(x):
    high = x.astype(BF16)
    rest = x - high.astype(F32)
    mid = rest.astype(BF16)
    low = (rest - mid.astype(F32)).astype(BF16)
    return high, mid, low


def planes_kernel(x_ref, out_ref):
    ib = x_ref.shape[1]
    rows = x_ref.shape[3]
    flat = out_ref.reshape(rows * ib, out_ref.shape[2])
    for i in range(ib):
        pair = jnp.concatenate([x_ref[0, i], x_ref[1, i]], axis=0)
        flat[pl.ds(i, rows, stride=ib), :] = pair.T


def planes_first(field, group):
    species, cells, points, planes = field.shape
    ib = 8
    return pl.pallas_call(
        planes_kernel,
        grid=(cells // ib,),
        in_specs=[pl.BlockSpec((2, ib, points, planes), lambda g: (group, g, 0, 0))],
        out_specs=pl.BlockSpec((planes, ib, 2 * points), lambda g: (0, g, 0)),
        out_shape=jax.ShapeDtypeStruct((planes, cells, 2 * points), F32),
        compiler_params=pltpu.CompilerParams(vmem_limit_bytes=VMEM_LIMIT),
        name="planes_first",
    )(field)


def lower_blocks(n):
    return [(r, c) for r in range(n) for c in range(r + 1)]


def store_lower(out_ref, main, cross):
    n = main.shape[0] // 128
    for b, (r, c) in enumerate(lower_blocks(n)):
        rs, cs = slice(128 * r, 128 * r + 128), slice(128 * c, 128 * c + 128)
        out_ref[128 * b : 128 * b + 128, :] = main[rs, cs] + cross[rs, cs] + cross[cs, rs].T


def gram_first_kernel(steps, ya_ref, yb_ref, out_ref, main, cross):
    step = pl.program_id(0)
    parts = [
        ref[:, 0, 0, tau].reshape(main.shape[0], 128) for ref in (ya_ref, yb_ref) for tau in range(2)
    ]
    high, low = split2(jnp.concatenate(parts, axis=1))
    mixed = dot16(high, low, NT)
    full = dot16(high, high, NT)

    @pl.when(step == 0)
    def _():
        main[...] = full
        cross[...] = mixed

    @pl.when(step > 0)
    def _():
        main[...] += full
        cross[...] += mixed

    @pl.when(step == steps - 1)
    def _():
        store_lower(out_ref, main, cross)


def gram_first(ya, yb, wide, narrow):
    size = wide * ya.shape[1]
    count = size // 128
    rows = 128 * (count * (count + 1) // 2)
    shape = (wide, 1, narrow, 2) + ya.shape[1:]
    spec = pl.BlockSpec((wide, 1, 1, 2) + ya.shape[1:], lambda g: (0, 0, g, 0, 0, 0))
    return pl.pallas_call(
        functools.partial(gram_first_kernel, narrow),
        grid=(narrow,),
        in_specs=[spec, spec],
        out_specs=pl.BlockSpec((rows, 128), lambda g: (0, 0)),
        out_shape=jax.ShapeDtypeStruct((rows, 128), F32),
        scratch_shapes=[pltpu.VMEM((size, size), F32), pltpu.VMEM((size, size), F32)],
        compiler_params=pltpu.CompilerParams(vmem_limit_bytes=VMEM_LIMIT),
        name="gram_first",
    )(ya.reshape(shape), yb.reshape(shape))


def summed_everywhere(packed, devices):
    rows = packed.shape[0]
    pieces = packed.reshape(devices, 1, rows * 128 // devices)
    own = jnp.sum(lax.all_to_all(pieces, ALL, 0, 0, tiled=True), axis=0)
    copies = jnp.broadcast_to(own[None], pieces.shape)
    return lax.all_to_all(copies, ALL, 0, 0, tiled=True).reshape(rows, 128)


NB = 16


def inverse_factor(gram):
    size = gram.shape[0]
    row = lax.broadcasted_iota(jnp.int32, (size, size), 0)
    col = lax.broadcasted_iota(jnp.int32, (size, size), 1)
    work = jnp.concatenate([gram, jnp.where(row == col, 1.0, 0.0).astype(F32)], axis=1)
    lane_row = lax.broadcasted_iota(jnp.int32, (NB, size), 0)
    done = []
    for b in range(size // NB):
        panel = work[:NB]
        left = size - NB * b
        cols = [
            jnp.broadcast_to(panel[:, NB * b + j : NB * b + j + 1], (NB, size)) for j in range(NB)
        ]
        pivots = jnp.ones((NB, size), F32)
        for k in range(NB):
            pivot = jnp.broadcast_to(cols[k][k : k + 1], (NB, size))
            ratio = jnp.where(lane_row > k, cols[k] * (1.0 / pivot), 0.0)
            for j in range(k + 1, NB):
                cols[j] = cols[j] - ratio * jnp.broadcast_to(cols[j][k : k + 1], (NB, size))
            both = jnp.concatenate([ratio, ratio], axis=1)
            panel = panel - both * jnp.broadcast_to(panel[k : k + 1], panel.shape)
            pivots = jnp.where(lane_row == k, pivot, pivots)
        scale = 1.0 / jnp.sqrt(pivots)
        panel = panel * jnp.concatenate([scale, scale], axis=1)
        done.append(panel[:, size:])
        if left > NB:
            high, mid, low = split3(panel)
            lhs = jnp.concatenate([high, high, high, mid, mid, low], axis=0)[:, :size]
            rhs = jnp.concatenate([high, mid, low, high, mid, high], axis=0)
            update = dot16(lhs, rhs, TN)
            work = work[NB:] - update[NB * (b + 1) :]
    return jnp.concatenate(done, axis=0)


def orthonormal_rows(rows):
    return dot32(inverse_factor(dot32(rows, rows, NT)), rows, NN)


def start_kernel(start_ref, out_ref):
    out_ref[...] = orthonormal_rows(start_ref[...].T)


def start_rows(start):
    return pl.pallas_call(
        start_kernel,
        out_shape=jax.ShapeDtypeStruct(start.shape[::-1], F32),
        compiler_params=pltpu.CompilerParams(vmem_limit_bytes=VMEM_LIMIT),
        name="start_rows",
    )(start)


def basis_kernel(packed_ref, start_ref, rows_ref, basis_ref, gram):
    n = gram.shape[0] // 128
    for b, (r, c) in enumerate(lower_blocks(n)):
        block = packed_ref[128 * b : 128 * b + 128, :]
        gram[128 * r : 128 * r + 128, 128 * c : 128 * c + 128] = block
        if r != c:
            gram[128 * c : 128 * c + 128, 128 * r : 128 * r + 128] = block.T

    def sweep(_, rows):
        return orthonormal_rows(dot32(rows, gram[...], NN))

    rows = lax.fori_loop(0, ITERS, sweep, start_ref[...])
    rows_ref[...] = rows
    basis_ref[...] = rows.T


def basis_rows(packed, start):
    rank, size = start.shape
    return pl.pallas_call(
        basis_kernel,
        out_shape=(
            jax.ShapeDtypeStruct((rank, size), F32),
            jax.ShapeDtypeStruct((size, rank), F32),
        ),
        scratch_shapes=[pltpu.VMEM((size, size), F32)],
        compiler_params=pltpu.CompilerParams(vmem_limit_bytes=VMEM_LIMIT),
        name="basis_rows",
    )(packed, start)


def reduce_kernel(rows_ref, ya_ref, yb_ref, red_ref, out_ref, main, cross):
    step = pl.program_id(0)
    rank = rows_ref.shape[0]

    bh, bl = split2(rows_ref[...])
    both = jnp.concatenate([bh, bl], axis=0)
    lane = lax.broadcasted_iota(jnp.int32, (rank, 128), 1)

    def work(y_ref):
        narrow = y_ref.shape[2]
        for m in range(narrow // 2):
            parts = [
                y_ref[:, 0, 2 * m + h, 0].reshape(rows_ref.shape[1], 128) for h in range(2)
            ]
            yh, yl = split2(jnp.concatenate(parts, axis=1))
            wide = dot16(both, yh, NN)
            got = wide[:rank] + (wide[rank:] + dot16(bh, yl, NN))
            a, b = got[:, :128], got[:, 128:]
            first = jnp.where(lane < 64, a, pltpu.roll(b, 64, 1))
            second = jnp.where(lane < 64, pltpu.roll(a, 64, 1), b)
            red_ref[0, 0, 0, :, 128 * m : 128 * m + 128] = first
            red_ref[0, 0, 1, :, 128 * m : 128 * m + 128] = second

    @pl.when(step < 2)
    def _():
        work(ya_ref)

    @pl.when(step >= 2)
    def _():
        work(yb_ref)

    stacked = jnp.concatenate([red_ref[0, 0, 0], red_ref[0, 0, 1]], axis=0)
    high, low = split2(stacked)
    full = dot16(high, high, TN)
    mixed = dot16(high, low, TN)

    @pl.when(step == 0)
    def _():
        main[...] = full
        cross[...] = mixed

    @pl.when(step > 0)
    def _():
        main[...] += full
        cross[...] += mixed

    @pl.when(step == 3)
    def _():
        store_lower(out_ref, main, cross)


def reduce_first(rows, ya, yb, wide, narrow):
    rank, size = rows.shape
    points = narrow * 64
    count = points // 128
    packed = 128 * (count * (count + 1) // 2)
    shape = (wide, 1, narrow, 2) + ya.shape[1:]
    block = (wide, 1, narrow, 1) + ya.shape[1:]
    return pl.pallas_call(
        reduce_kernel,
        grid=(4,),
        in_specs=[
            pl.BlockSpec((rank, size), lambda g: (0, 0)),
            pl.BlockSpec(block, lambda g: (0, 0, 0, jnp.minimum(g, 1), 0, 0)),
            pl.BlockSpec(block, lambda g: (0, 0, 0, jnp.maximum(g, 2) - 2, 0, 0)),
        ],
        out_specs=(
            pl.BlockSpec((1, 1, 2, rank, points), lambda g: (g // 2, g % 2, 0, 0, 0)),
            pl.BlockSpec((packed, 128), lambda g: (0, 0)),
        ),
        out_shape=(
            jax.ShapeDtypeStruct((2, 2, 2, rank, points), F32),
            jax.ShapeDtypeStruct((packed, 128), F32),
        ),
        scratch_shapes=[pltpu.VMEM((points, points), F32), pltpu.VMEM((points, points), F32)],
        compiler_params=pltpu.CompilerParams(vmem_limit_bytes=VMEM_LIMIT),
        name="reduce_first",
    )(rows, ya.reshape(shape), yb.reshape(shape))


def core_kernel(rows_ref, red_ref, out_ref):
    rank = rows_ref.shape[0]
    bh, bl = split2(rows_ref[...])
    both = jnp.concatenate([bh, bl], axis=0)
    for s in range(2):
        rh, rl = split2(red_ref[0, 0, s])
        wide = dot16(rh, both, NT)
        got = wide[:, :rank] + (wide[:, rank:] + dot16(rl, bh, NT))
        out_ref[:, 0, s] = got.reshape(out_ref.shape[0], got.shape[0] // out_ref.shape[0], rank)


def core_blocks(rows, red, narrow):
    rank, points = rows.shape
    per = red.shape[3] // narrow
    return pl.pallas_call(
        core_kernel,
        grid=(4,),
        in_specs=[
            pl.BlockSpec((rank, points), lambda g: (0, 0)),
            pl.BlockSpec((1, 1, 2, red.shape[3], points), lambda g: (g // 2, g % 2, 0, 0, 0)),
        ],
        out_specs=pl.BlockSpec((narrow, 1, 2, per, rank), lambda g: (0, g % 2, g // 2, 0, 0)),
        out_shape=jax.ShapeDtypeStruct((narrow, 2, 4, per, rank), F32),
        compiler_params=pltpu.CompilerParams(vmem_limit_bytes=VMEM_LIMIT),
        name="core_blocks",
    )(rows, red)


def local(field, start_first, start_second):
    wide, narrow = lax.axis_size("wide"), lax.axis_size("narrow")
    ya = lax.all_to_all(planes_first(field, 0), ALL, 0, 0, tiled=True)
    yb = lax.all_to_all(planes_first(field, 1), ALL, 0, 0, tiled=True)
    rows_first = start_rows(start_first)
    rows_second = start_rows(start_second)
    packed = summed_everywhere(gram_first(ya, yb, wide, narrow), wide * narrow)
    rows_first, basis_first = basis_rows(packed, rows_first)
    red, packed = reduce_first(rows_first, ya, yb, wide, narrow)
    packed = summed_everywhere(packed, wide * narrow)
    rows_second, basis_second = basis_rows(packed, rows_second)
    core = core_blocks(rows_second, red, narrow)
    core = lax.all_to_all(core, "narrow", 0, 0, tiled=True)
    core = core.reshape(2 * narrow, *core.shape[2:])
    return (core, basis_first, basis_second)


def solution(mesh):
    placed = (P(None, "wide", "narrow", None), P(), P())
    return jax.shard_map(
        local,
        mesh=mesh,
        in_specs=placed,
        out_specs=(P("wide", None, "narrow", None), P(), P()),
        check_vma=False,
    )
```

```python
import functools
import jax
import jax.numpy as jnp
from jax import lax
from jax.experimental import pallas as pl
from jax.experimental.pallas import tpu as pltpu
from jax.sharding import PartitionSpec as P

ITERS = 3
F32 = jnp.float32
BF16 = jnp.bfloat16
EXACT = lax.Precision.HIGHEST
ALL = ("wide", "narrow")
MIB = 1024 * 1024

NN = (((1,), (0,)), ((), ()))
NT = (((1,), (1,)), ((), ()))
TN = (((0,), (0,)), ((), ()))


def dot32(a, b, dims):
    return lax.dot_general(a, b, dims, precision=EXACT, preferred_element_type=F32)


def dot16(a, b, dims):
    return lax.dot_general(a, b, dims, preferred_element_type=F32)


def split2(x):
    high = x.astype(BF16)
    low = (x - high.astype(F32)).astype(BF16)
    return high, low


def split3(x):
    high = x.astype(BF16)
    rest = x - high.astype(F32)
    mid = rest.astype(BF16)
    low = (rest - mid.astype(F32)).astype(BF16)
    return high, mid, low


def planes_kernel(x_ref, out_ref):
    ib = x_ref.shape[1]
    rows = x_ref.shape[3]
    flat = out_ref.reshape(rows * ib, out_ref.shape[2])
    for i in range(ib):
        pair = jnp.concatenate([x_ref[0, i], x_ref[1, i]], axis=0)
        flat[pl.ds(i, rows, stride=ib), :] = pair.T


def planes_first(field):
    species, cells, points, planes = field.shape
    ib = 8
    blocks = cells // ib
    return pl.pallas_call(
        planes_kernel,
        grid=(species // 2, blocks),
        in_specs=[pl.BlockSpec((2, ib, points, planes), lambda c, g: (c, g, 0, 0))],
        out_specs=pl.BlockSpec((planes, ib, 2 * points), lambda c, g: (0, c * blocks + g, 0)),
        out_shape=jax.ShapeDtypeStruct((planes, cells * species // 2, 2 * points), F32),
        compiler_params=pltpu.CompilerParams(vmem_limit_bytes=60 * MIB),
        name="planes_first",
    )(field)


def lower_blocks(n):
    return [(r, c) for r in range(n) for c in range(r + 1)]


def store_lower(out_ref, main, cross):
    n = main.shape[0] // 128
    for b, (r, c) in enumerate(lower_blocks(n)):
        rs, cs = slice(128 * r, 128 * r + 128), slice(128 * c, 128 * c + 128)
        out_ref[128 * b : 128 * b + 128, :] = main[rs, cs] + cross[rs, cs] + cross[cs, rs].T


def gram_first_kernel(steps, y_ref, out_ref, main, cross):
    step = pl.program_id(0)
    size = main.shape[0]
    parts = [
        y_ref[:, n, tau, c].reshape(size, 128)
        for n in range(y_ref.shape[1])
        for tau in range(2)
        for c in range(2)
    ]
    high, low = split2(jnp.concatenate(parts, axis=1))
    mixed = dot16(high, low, NT)
    full = dot16(high, high, NT)

    @pl.when(step == 0)
    def _():
        main[...] = full
        cross[...] = mixed

    @pl.when(step > 0)
    def _():
        main[...] += full
        cross[...] += mixed

    @pl.when(step == steps - 1)
    def _():
        store_lower(out_ref, main, cross)


GRAM_POINTS = 2


def gram_first(y):
    wide, narrow, _, groups, cells, lanes = y.shape
    size = wide * cells
    count = size // 128
    rows = 128 * (count * (count + 1) // 2)
    steps = narrow // GRAM_POINTS
    return pl.pallas_call(
        functools.partial(gram_first_kernel, steps),
        grid=(steps,),
        in_specs=[
            pl.BlockSpec(
                (wide, GRAM_POINTS, 2, groups, cells, lanes), lambda g: (0, g, 0, 0, 0, 0)
            )
        ],
        out_specs=pl.BlockSpec((rows, 128), lambda g: (0, 0)),
        out_shape=jax.ShapeDtypeStruct((rows, 128), F32),
        scratch_shapes=[pltpu.VMEM((size, size), F32), pltpu.VMEM((size, size), F32)],
        compiler_params=pltpu.CompilerParams(vmem_limit_bytes=60 * MIB),
        name="gram_first",
    )(y)


def summed_pieces(packed, devices):
    pieces = packed.reshape(devices, 1, packed.shape[0] * 128 // devices)
    return jnp.sum(lax.all_to_all(pieces, ALL, 0, 0, tiled=True), axis=0)


def gathered_pieces(own, devices):
    copies = jnp.broadcast_to(own[None], (devices, *own.shape))
    return lax.all_to_all(copies, ALL, 0, 0, tiled=True).reshape(-1, 128)


WINDOW, PANEL = 32, 16


def inverse_factor(gram):
    size = gram.shape[0]
    row = lax.broadcasted_iota(jnp.int32, (size, size), 0)
    col = lax.broadcasted_iota(jnp.int32, (size, size), 1)
    work = jnp.concatenate([gram, jnp.where(row == col, 1.0, 0.0).astype(F32)], axis=1)
    low = lax.broadcasted_iota(jnp.int32, (8, size), 0)
    blocks = WINDOW // 8

    def spread(x):
        return jnp.broadcast_to(x, (8, x.shape[1]))

    done, scales = [], []
    for base in range(0, size, WINDOW):
        rows = [work[8 * i : 8 * i + 8] for i in range(blocks)]
        inverses, pivots = [None] * blocks, [None] * blocks
        for first in range(0, WINDOW, PANEL):
            cols = {}
            for j in range(PANEL):
                c = base + first + j
                for i in range(first // 8, blocks):
                    cols[j, i] = jnp.broadcast_to(rows[i][:, c : c + 1], (8, size))
            for k in range(PANEL):
                here, at = (first + k) // 8, k % 8
                pivot = spread(cols[k, here][at : at + 1])
                inverse = 1.0 / pivot
                ratio = {i: cols[k, i] * inverse for i in range(here, blocks)}
                ratio[here] = jnp.where(low > at, ratio[here], 0.0)
                for j in range(k + 1, PANEL):
                    piece = spread(cols[j, here][at : at + 1])
                    for i in range(here, blocks):
                        cols[j, i] = cols[j, i] - ratio[i] * piece
                piece = spread(rows[here][at : at + 1])
                for i in range(here, blocks):
                    rows[i] = rows[i] - jnp.concatenate([ratio[i], ratio[i]], axis=1) * piece
                inverses[here] = jnp.where(low == at, inverse, inverses[here]) if at else inverse
                pivots[here] = jnp.where(low == at, pivot, pivots[here]) if at else pivot
        done += [r[:, size:] for r in rows]
        scales += pivots
        if base + WINDOW < size:
            left = [r[:, :size] * s for r, s in zip(rows, inverses)]
            lh, lm, ll = split3(jnp.concatenate(left, axis=0))
            rh, rm, rl = split3(jnp.concatenate(rows, axis=0))
            lhs = jnp.concatenate([lh, lh, lh, lm, lm, ll], axis=0)
            rhs = jnp.concatenate([rh, rm, rl, rh, rm, rh], axis=0)
            work = work[WINDOW:] - dot16(lhs, rhs, TN)[base + WINDOW :]
    return jnp.concatenate([d * (1.0 / jnp.sqrt(p)) for d, p in zip(done, scales)], axis=0)


def orthonormal_rows(rows):
    return dot32(inverse_factor(dot32(rows, rows, NT)), rows, NN)


def start_kernel(start_ref, out_ref):
    out_ref[...] = orthonormal_rows(start_ref[...].T)


def start_rows(start):
    return pl.pallas_call(
        start_kernel,
        out_shape=jax.ShapeDtypeStruct(start.shape[::-1], F32),
        compiler_params=pltpu.CompilerParams(vmem_limit_bytes=8 * MIB),
        name="start_rows",
    )(start)


def basis_kernel(packed_ref, start_ref, rows_ref, basis_ref, gram):
    n = gram.shape[0] // 128
    for b, (r, c) in enumerate(lower_blocks(n)):
        block = packed_ref[128 * b : 128 * b + 128, :]
        gram[128 * r : 128 * r + 128, 128 * c : 128 * c + 128] = block
        if r != c:
            gram[128 * c : 128 * c + 128, 128 * r : 128 * r + 128] = block.T

    def sweep(_, rows):
        return orthonormal_rows(dot32(rows, gram[...], NN))

    rows = lax.fori_loop(0, ITERS, sweep, start_ref[...])
    rows_ref[...] = rows
    basis_ref[...] = rows.T


def basis_rows(packed, start):
    rank, size = start.shape
    return pl.pallas_call(
        basis_kernel,
        out_shape=(
            jax.ShapeDtypeStruct((rank, size), F32),
            jax.ShapeDtypeStruct((size, rank), F32),
        ),
        scratch_shapes=[pltpu.VMEM((size, size), F32)],
        compiler_params=pltpu.CompilerParams(vmem_limit_bytes=10 * MIB),
        name="basis_rows",
    )(packed, start)


def reduce_kernel(me_ref, rows_ref, y_ref, *refs):
    *out_refs, packed_ref, reduced, main, cross = refs
    step = pl.program_id(0)
    rank, size = rows_ref.shape
    narrow = len(out_refs)
    per = rank // narrow
    bh, bl = split2(rows_ref[...])
    both = jnp.concatenate([bh, bl], axis=0)
    lane = lax.broadcasted_iota(jnp.int32, (rank, 128), 1)
    for m in range(narrow // 2):
        parts = [y_ref[:, 2 * m + h, 0, 0].reshape(size, 128) for h in range(2)]
        yh, yl = split2(jnp.concatenate(parts, axis=1))
        wide = dot16(both, yh, NN)
        got = wide[:rank] + (wide[rank:] + dot16(bh, yl, NN))
        a, b = got[:, :128], got[:, 128:]
        lanes = slice(128 * m, 128 * m + 128)
        reduced[:rank, lanes] = jnp.where(lane < 64, a, pltpu.roll(b, 64, 1))
        reduced[rank:, lanes] = jnp.where(lane < 64, pltpu.roll(a, 64, 1), b)
    for j, out_ref in enumerate(out_refs):
        owner = lax.rem(me_ref[0] + j, narrow)
        for s in range(2):
            start = pl.multiple_of(rank * s + owner * per, per)
            out_ref[0, s] = reduced[pl.ds(start, per), :]
    high, low = split2(reduced[...])
    full = dot16(high, high, TN)
    mixed = dot16(high, low, TN)

    @pl.when(step == 0)
    def _():
        main[...] = full
        cross[...] = mixed

    @pl.when(step > 0)
    def _():
        main[...] += full
        cross[...] += mixed

    @pl.when(step == 3)
    def _():
        store_lower(packed_ref, main, cross)


def reduce_first(me, rows, y):
    wide, narrow, _, groups, cells, lanes = y.shape
    rank, size = rows.shape
    points = narrow * 64
    count = points // 128
    packed = 128 * (count * (count + 1) // 2)
    per = rank // narrow
    *blocks, gram = pl.pallas_call(
        reduce_kernel,
        grid=(2 * groups,),
        in_specs=[
            pl.BlockSpec(memory_space=pltpu.SMEM),
            pl.BlockSpec((rank, size), lambda g: (0, 0)),
            pl.BlockSpec((wide, narrow, 1, 1, cells, lanes), lambda g: (0, 0, g % 2, g // 2, 0, 0)),
        ],
        out_specs=[pl.BlockSpec((1, 2, per, points), lambda g: (g, 0, 0, 0))] * narrow
        + [pl.BlockSpec((packed, 128), lambda g: (0, 0))],
        out_shape=[jax.ShapeDtypeStruct((2 * groups, 2, per, points), F32)] * narrow
        + [jax.ShapeDtypeStruct((packed, 128), F32)],
        scratch_shapes=[
            pltpu.VMEM((2 * rank, points), F32),
            pltpu.VMEM((points, points), F32),
            pltpu.VMEM((points, points), F32),
        ],
        compiler_params=pltpu.CompilerParams(vmem_limit_bytes=60 * MIB),
        name="reduce_first",
    )(me, rows, y)
    return blocks, gram


def core_kernel(me_ref, basis_ref, *refs):
    *block_refs, out_ref = refs
    narrow = len(block_refs)
    taus, lows, per, points = block_refs[0].shape
    rank = basis_ref.shape[1]
    count = taus * lows * per
    bh, bl = split2(basis_ref[...])
    both = jnp.concatenate([bh, bl], axis=1)
    rows = jnp.concatenate([r[...].reshape(count, points) for r in block_refs], axis=0)
    rh, rl = split2(rows)
    wide = dot16(rh, both, NN)
    got = wide[:, :rank] + (wide[:, rank:] + dot16(rl, bh, NN))
    for j in range(narrow):
        source = lax.rem(me_ref[0] + (narrow - j), narrow)
        block = got[count * j : count * (j + 1)].reshape(taus, lows, per, rank)
        for tau in range(taus):
            out_ref[taus * source + tau] = block[tau]


def core_blocks(me, basis, blocks):
    points, rank = basis.shape
    narrow = len(blocks)
    steps, lows, per, _ = blocks[0].shape
    groups = steps // 2
    return pl.pallas_call(
        core_kernel,
        grid=(groups,),
        in_specs=[
            pl.BlockSpec(memory_space=pltpu.SMEM),
            pl.BlockSpec((points, rank), lambda g: (0, 0)),
        ]
        + [pl.BlockSpec((2, lows, per, points), lambda g: (g, 0, 0, 0))] * narrow,
        out_specs=pl.BlockSpec((2 * narrow, lows, per, rank), lambda g: (0, g, 0, 0)),
        out_shape=jax.ShapeDtypeStruct((2 * narrow, groups * lows, per, rank), F32),
        compiler_params=pltpu.CompilerParams(vmem_limit_bytes=12 * MIB),
        name="core_blocks",
    )(me, basis, *blocks)


def local(field, start_first, start_second):
    wide, narrow = lax.axis_size("wide"), lax.axis_size("narrow")
    devices = wide * narrow
    me = lax.axis_index("narrow").astype(jnp.int32).reshape(1)
    planes = lax.all_to_all(planes_first(field), ALL, 0, 0, tiled=True)
    y = planes.reshape(wide, narrow, 2, field.shape[0] // 2, field.shape[1], planes.shape[2])
    rows_first = start_rows(start_first)
    rows_second = start_rows(start_second)
    packed = gathered_pieces(summed_pieces(gram_first(y), devices), devices)
    rows_first, basis_first = basis_rows(packed, rows_first)
    blocks, packed = reduce_first(me, rows_first, y)
    own, blocks = lax.optimization_barrier((summed_pieces(packed, devices), blocks))
    blocks = [blocks[0]] + [
        lax.ppermute(blocks[j], "narrow", [(n, (n + j) % narrow) for n in range(narrow)])
        for j in range(1, narrow)
    ]
    _, basis_second = basis_rows(gathered_pieces(own, devices), rows_second)
    core = core_blocks(me, basis_second, blocks)
    return (core, basis_first, basis_second)


def solution(mesh):
    placed = (P(None, "wide", "narrow", None), P(), P())
    return jax.shard_map(
        local,
        mesh=mesh,
        in_specs=placed,
        out_specs=(P("wide", None, "narrow", None), P(), P()),
        check_vma=False,
    )
```

```python
import functools
import jax
import jax.numpy as jnp
from jax import lax
from jax.experimental import pallas as pl
from jax.experimental.pallas import tpu as pltpu
from jax.sharding import Mesh, PartitionSpec as P

ITERS = 3
F32 = jnp.float32
BF16 = jnp.bfloat16
EXACT = lax.Precision.HIGHEST
ALL = ("board", "core", "narrow")
CHIPS = ("board", "narrow")
SWAP = [(0, 1), (1, 0)]
MIB = 1024 * 1024

NN = (((1,), (0,)), ((), ()))
NT = (((1,), (1,)), ((), ()))
TN = (((0,), (0,)), ((), ()))


def dot32(a, b, dims):
    return lax.dot_general(a, b, dims, precision=EXACT, preferred_element_type=F32)


def dot16(a, b, dims):
    return lax.dot_general(a, b, dims, preferred_element_type=F32)


def split2(x):
    high = x.astype(BF16)
    low = (x - high.astype(F32)).astype(BF16)
    return high, low


def split3(x):
    high = x.astype(BF16)
    rest = x - high.astype(F32)
    mid = rest.astype(BF16)
    low = (rest - mid.astype(F32)).astype(BF16)
    return high, mid, low


def planes_kernel(me_ref, core_ref, x_ref, out_ref):
    ib = x_ref.shape[1]
    rows = x_ref.shape[3]
    flat = out_ref.reshape(rows * ib, out_ref.shape[2])
    for i in range(ib):
        pair = jnp.concatenate([x_ref[0, i], x_ref[1, i]], axis=0)
        flat[pl.ds(i, rows, stride=ib), :] = pair.T


def planes_first(me, core, field):
    species, cells, points, planes = field.shape
    ib = 8
    blocks = cells // ib
    return pl.pallas_call(
        planes_kernel,
        grid=(species // 2, blocks),
        in_specs=[pl.BlockSpec(memory_space=pltpu.SMEM)] * 2
        + [pl.BlockSpec((2, ib, points, planes), lambda c, g: (c, g, 0, 0))],
        out_specs=pl.BlockSpec((planes, ib, 2 * points), lambda c, g: (0, c * blocks + g, 0)),
        out_shape=jax.ShapeDtypeStruct((planes, cells * species // 2, 2 * points), F32),
        compiler_params=pltpu.CompilerParams(vmem_limit_bytes=60 * MIB),
        name="planes_first",
    )(me, core, field)


def lower_blocks(n):
    return [(r, c) for r in range(n) for c in range(r + 1)]


def store_lower(core_ref, keep_ref, send_ref, packed, main, cross):
    n = main.shape[0] // 128
    for b, (r, c) in enumerate(lower_blocks(n)):
        rs, cs = slice(128 * r, 128 * r + 128), slice(128 * c, 128 * c + 128)
        packed[128 * b : 128 * b + 128, :] = main[rs, cs] + cross[rs, cs] + cross[cs, rs].T
    half = keep_ref.shape[0]
    keep_ref[...] = packed[pl.ds(pl.multiple_of(core_ref[0] * half, half), half), :]
    send_ref[...] = packed[pl.ds(pl.multiple_of((1 - core_ref[0]) * half, half), half), :]


def gram_first_kernel(steps, core_ref, y_ref, keep_ref, send_ref, packed, main, cross):
    step = pl.program_id(0)
    size = main.shape[0]
    parts = [
        y_ref[:, n, tau, c].reshape(size, 128)
        for n in range(y_ref.shape[1])
        for tau in range(2)
        for c in range(2)
    ]
    high, low = split2(jnp.concatenate(parts, axis=1))
    mixed = dot16(high, low, NT)
    full = dot16(high, high, NT)

    @pl.when(step == 0)
    def _():
        main[...] = full
        cross[...] = mixed

    @pl.when(step > 0)
    def _():
        main[...] += full
        cross[...] += mixed

    @pl.when(step == steps - 1)
    def _():
        store_lower(core_ref, keep_ref, send_ref, packed, main, cross)


GRAM_POINTS = 2


def gram_first(core, y):
    wide, narrow, _, groups, cells, lanes = y.shape
    size = wide * cells
    count = size // 128
    rows = 128 * (count * (count + 1) // 2)
    steps = narrow // GRAM_POINTS
    return pl.pallas_call(
        functools.partial(gram_first_kernel, steps),
        grid=(steps,),
        in_specs=[
            pl.BlockSpec(memory_space=pltpu.SMEM),
            pl.BlockSpec(
                (wide, GRAM_POINTS, 2, groups, cells, lanes), lambda g: (0, g, 0, 0, 0, 0)
            ),
        ],
        out_specs=[pl.BlockSpec((rows // 2, 128), lambda g: (0, 0))] * 2,
        out_shape=[jax.ShapeDtypeStruct((rows // 2, 128), F32)] * 2,
        scratch_shapes=[
            pltpu.VMEM((rows, 128), F32),
            pltpu.VMEM((size, size), F32),
            pltpu.VMEM((size, size), F32),
        ],
        compiler_params=pltpu.CompilerParams(vmem_limit_bytes=50 * MIB),
        name="gram_first",
    )(core, y)


def summed_pieces(keep, send, chips):
    half = keep + lax.ppermute(send, "core", SWAP)
    pieces = half.reshape(chips, 1, half.shape[0] * 128 // chips)
    return jnp.sum(lax.all_to_all(pieces, CHIPS, 0, 0, tiled=True), axis=0)


def gathered_half(own, chips):
    copies = jnp.broadcast_to(own[None], (chips, *own.shape))
    return lax.all_to_all(copies, CHIPS, 0, 0, tiled=True).reshape(-1, 128)


def swapped(mine):
    return lax.ppermute(mine, "core", SWAP)


WINDOW, PANEL = 32, 16


def inverse_factor(gram):
    size = gram.shape[0]
    row = lax.broadcasted_iota(jnp.int32, (size, size), 0)
    col = lax.broadcasted_iota(jnp.int32, (size, size), 1)
    work = jnp.concatenate([gram, jnp.where(row == col, 1.0, 0.0).astype(F32)], axis=1)
    low = lax.broadcasted_iota(jnp.int32, (8, size), 0)
    blocks = WINDOW // 8

    def spread(x):
        return jnp.broadcast_to(x, (8, x.shape[1]))

    done, scales = [], []
    for base in range(0, size, WINDOW):
        rows = [work[8 * i : 8 * i + 8] for i in range(blocks)]
        inverses, pivots = [None] * blocks, [None] * blocks
        for first in range(0, WINDOW, PANEL):
            cols = {}
            for j in range(PANEL):
                c = base + first + j
                for i in range(first // 8, blocks):
                    cols[j, i] = jnp.broadcast_to(rows[i][:, c : c + 1], (8, size))
            for k in range(PANEL):
                here, at = (first + k) // 8, k % 8
                pivot = spread(cols[k, here][at : at + 1])
                inverse = 1.0 / pivot
                ratio = {i: cols[k, i] * inverse for i in range(here, blocks)}
                ratio[here] = jnp.where(low > at, ratio[here], 0.0)
                for j in range(k + 1, PANEL):
                    piece = spread(cols[j, here][at : at + 1])
                    for i in range(here, blocks):
                        cols[j, i] = cols[j, i] - ratio[i] * piece
                piece = spread(rows[here][at : at + 1])
                for i in range(here, blocks):
                    rows[i] = rows[i] - jnp.concatenate([ratio[i], ratio[i]], axis=1) * piece
                inverses[here] = jnp.where(low == at, inverse, inverses[here]) if at else inverse
                pivots[here] = jnp.where(low == at, pivot, pivots[here]) if at else pivot
        done += [r[:, size:] for r in rows]
        scales += pivots
        if base + WINDOW < size:
            left = [r[:, :size] * s for r, s in zip(rows, inverses)]
            lh, lm, ll = split3(jnp.concatenate(left, axis=0))
            rh, rm, rl = split3(jnp.concatenate(rows, axis=0))
            lhs = jnp.concatenate([lh, lh, lh, lm, lm, ll], axis=0)
            rhs = jnp.concatenate([rh, rm, rl, rh, rm, rh], axis=0)
            work = work[WINDOW:] - dot16(lhs, rhs, TN)[base + WINDOW :]
    return jnp.concatenate([d * (1.0 / jnp.sqrt(p)) for d, p in zip(done, scales)], axis=0)


def orthonormal_rows(rows):
    rank = rows.shape[0]
    h, m, l = split3(rows)
    stack = jnp.concatenate([h, m, l], axis=0)
    d = dot16(stack, stack, NT)
    a, b = slice(0, rank), slice(rank, 2 * rank)
    c = slice(2 * rank, 3 * rank)
    gram = d[a, a] + (d[a, b] + d[b, a]) + (d[b, b] + (d[a, c] + d[c, a]))
    th, tm, tl = split3(inverse_factor(gram))
    return dot16(
        jnp.concatenate([th, th, th, tm, tm, tl], axis=1),
        jnp.concatenate([h, m, l, h, m, h], axis=0),
        NN,
    )


def start_kernel(start_ref, out_ref):
    out_ref[...] = orthonormal_rows(start_ref[...].T)


def start_rows(start):
    return pl.pallas_call(
        start_kernel,
        out_shape=jax.ShapeDtypeStruct(start.shape[::-1], F32),
        compiler_params=pltpu.CompilerParams(vmem_limit_bytes=8 * MIB),
        name="start_rows",
    )(start)


def basis_kernel(core_ref, mine_ref, other_ref, start_ref, rows_ref, basis_ref, packed, gram):
    half = mine_ref.shape[0]
    packed[pl.ds(pl.multiple_of(core_ref[0] * half, half), half), :] = mine_ref[...]
    packed[pl.ds(pl.multiple_of((1 - core_ref[0]) * half, half), half), :] = other_ref[...]
    n = gram.shape[0] // 128
    for b, (r, c) in enumerate(lower_blocks(n)):
        rs, cs = slice(128 * r, 128 * r + 128), slice(128 * c, 128 * c + 128)
        block = packed[128 * b : 128 * b + 128, :]
        gram[rs, cs] = block
        if r != c:
            gram[cs, rs] = block.T

    def sweep(_, rows):
        return orthonormal_rows(dot32(rows, gram[...], NN))

    rows = lax.fori_loop(0, ITERS, sweep, start_ref[...])
    rows_ref[...] = rows
    basis_ref[...] = rows.T


def basis_rows(core, mine, other, start):
    rank, size = start.shape
    whole = pl.BlockSpec(memory_space=pltpu.VMEM)
    return pl.pallas_call(
        basis_kernel,
        in_specs=[pl.BlockSpec(memory_space=pltpu.SMEM), whole, whole, whole],
        out_shape=(
            jax.ShapeDtypeStruct((rank, size), F32),
            jax.ShapeDtypeStruct((size, rank), F32),
        ),
        scratch_shapes=[
            pltpu.VMEM((2 * mine.shape[0], 128), F32),
            pltpu.VMEM((size, size), F32),
        ],
        compiler_params=pltpu.CompilerParams(vmem_limit_bytes=16 * MIB),
        name="basis_rows",
    )(core, mine, other, start)


def reduce_kernel(me_ref, core_ref, rows_ref, y_ref, *refs):
    *out_refs, keep_ref, send_ref, packed, reduced, main, cross = refs
    step = pl.program_id(0)
    rank, size = rows_ref.shape
    narrow = len(out_refs)
    per = rank // narrow
    bh, bl = split2(rows_ref[...])
    both = jnp.concatenate([bh, bl], axis=0)
    lane = lax.broadcasted_iota(jnp.int32, (rank, 128), 1)
    for m in range(narrow // 2):
        parts = [y_ref[:, 2 * m + h, 0, 0].reshape(size, 128) for h in range(2)]
        yh, yl = split2(jnp.concatenate(parts, axis=1))
        wide = dot16(both, yh, NN)
        got = wide[:rank] + (wide[rank:] + dot16(bh, yl, NN))
        a, b = got[:, :128], got[:, 128:]
        lanes = slice(128 * m, 128 * m + 128)
        reduced[:rank, lanes] = jnp.where(lane < 64, a, pltpu.roll(b, 64, 1))
        reduced[rank:, lanes] = jnp.where(lane < 64, pltpu.roll(a, 64, 1), b)
    for j, out_ref in enumerate(out_refs):
        owner = lax.rem(me_ref[0] + j, narrow)
        for s in range(2):
            start = pl.multiple_of(rank * s + owner * per, per)
            out_ref[0, s] = reduced[pl.ds(start, per), :]
    high, low = split2(reduced[...])
    full = dot16(high, high, TN)
    mixed = dot16(high, low, TN)

    @pl.when(step == 0)
    def _():
        main[...] = full
        cross[...] = mixed

    @pl.when(step > 0)
    def _():
        main[...] += full
        cross[...] += mixed

    @pl.when(step == 3)
    def _():
        store_lower(core_ref, keep_ref, send_ref, packed, main, cross)


def reduce_first(me, core, rows, y):
    wide, narrow, _, groups, cells, lanes = y.shape
    rank, size = rows.shape
    points = narrow * 64
    count = points // 128
    packed = 128 * (count * (count + 1) // 2)
    per = rank // narrow
    *blocks, keep, send = pl.pallas_call(
        reduce_kernel,
        grid=(2 * groups,),
        in_specs=[
            pl.BlockSpec(memory_space=pltpu.SMEM),
            pl.BlockSpec(memory_space=pltpu.SMEM),
            pl.BlockSpec((rank, size), lambda g: (0, 0)),
            pl.BlockSpec((wide, narrow, 1, 1, cells, lanes), lambda g: (0, 0, g % 2, g // 2, 0, 0)),
        ],
        out_specs=[pl.BlockSpec((1, 2, per, points), lambda g: (g, 0, 0, 0))] * narrow
        + [pl.BlockSpec((packed // 2, 128), lambda g: (0, 0))] * 2,
        out_shape=[jax.ShapeDtypeStruct((2 * groups, 2, per, points), F32)] * narrow
        + [jax.ShapeDtypeStruct((packed // 2, 128), F32)] * 2,
        scratch_shapes=[
            pltpu.VMEM((packed, 128), F32),
            pltpu.VMEM((2 * rank, points), F32),
            pltpu.VMEM((points, points), F32),
            pltpu.VMEM((points, points), F32),
        ],
        compiler_params=pltpu.CompilerParams(vmem_limit_bytes=48 * MIB),
        name="reduce_first",
    )(me, core, rows, y)
    return blocks, keep, send


def core_kernel(me_ref, rows_ref, *refs):
    *block_refs, out_ref = refs
    narrow = len(block_refs)
    taus, lows, per, points = block_refs[0].shape
    rank = rows_ref.shape[0]
    count = taus * lows * per
    bh, bl = split2(rows_ref[...])
    both = jnp.concatenate([bh, bl], axis=0)
    rows = jnp.concatenate([r[...].reshape(count, points) for r in block_refs], axis=0)
    rh, rl = split2(rows)
    wide = dot16(rh, both, NT)
    got = wide[:, :rank] + (wide[:, rank:] + dot16(rl, bh, NT))
    for j in range(narrow):
        source = lax.rem(me_ref[0] + (narrow - j), narrow)
        block = got[count * j : count * (j + 1)].reshape(taus, lows, per, rank)
        for tau in range(taus):
            out_ref[taus * source + tau] = block[tau]


def core_blocks(me, rows, blocks):
    rank, points = rows.shape
    narrow = len(blocks)
    steps, lows, per, _ = blocks[0].shape
    groups = steps // 2
    return pl.pallas_call(
        core_kernel,
        grid=(groups,),
        in_specs=[
            pl.BlockSpec(memory_space=pltpu.SMEM),
            pl.BlockSpec((rank, points), lambda g: (0, 0)),
        ]
        + [pl.BlockSpec((2, lows, per, points), lambda g: (g, 0, 0, 0))] * narrow,
        out_specs=pl.BlockSpec((2 * narrow, lows, per, rank), lambda g: (0, g, 0, 0)),
        out_shape=jax.ShapeDtypeStruct((2 * narrow, groups * lows, per, rank), F32),
        compiler_params=pltpu.CompilerParams(vmem_limit_bytes=12 * MIB),
        name="core_blocks",
    )(me, rows, *blocks)


def whole(field, start_first, start_second):
    narrow = lax.axis_size("narrow")
    wide = lax.axis_size("board") * lax.axis_size("core")
    chips = lax.axis_size("board") * narrow
    me = lax.axis_index("narrow").astype(jnp.int32).reshape(1)
    core = lax.axis_index("core").astype(jnp.int32).reshape(1)
    planes = lax.all_to_all(planes_first(me, core, field), ALL, 0, 0, tiled=True)
    y = planes.reshape(wide, narrow, 2, field.shape[0] // 2, field.shape[1], planes.shape[2])
    rows_first = start_rows(start_first)
    rows_second = start_rows(start_second)
    own = summed_pieces(*gram_first(core, y), chips)
    mine = gathered_half(own, chips)
    rows_first, basis_first = basis_rows(core, mine, swapped(mine), rows_first)
    blocks, keep, send = reduce_first(me, core, rows_first, y)
    own, blocks = lax.optimization_barrier((summed_pieces(keep, send, chips), blocks))
    moved = [
        lax.ppermute(blocks[j], "narrow", [(n, (n + j) % narrow) for n in range(narrow)])
        for j in range(1, narrow)
    ]
    mine = gathered_half(own, chips)
    rows_second, basis_second = basis_rows(core, mine, swapped(mine), rows_second)
    return (core_blocks(me, rows_second, [blocks[0]] + moved), basis_first, basis_second)


def solution(mesh):
    wide, narrow = mesh.devices.shape
    finer = Mesh(mesh.devices.reshape(wide // 2, 2, narrow), ALL)
    first = ("board", "core")
    return jax.shard_map(
        whole,
        mesh=finer,
        in_specs=(P(None, first, "narrow", None), P(), P()),
        out_specs=(P(first, None, "narrow", None), P(), P()),
        check_vma=False,
    )
```

```python
import functools
import jax
import jax.numpy as jnp
from jax import lax
from jax.experimental import pallas as pl
from jax.experimental.pallas import tpu as pltpu
from jax.sharding import Mesh, PartitionSpec as P

ITERS = 3
F32 = jnp.float32
BF16 = jnp.bfloat16
EXACT = lax.Precision.HIGHEST
ALL = ("board", "core", "narrow")
CHIPS = ("board", "narrow")
SWAP = [(0, 1), (1, 0)]
MIB = 1024 * 1024

NN = (((1,), (0,)), ((), ()))
NT = (((1,), (1,)), ((), ()))
TN = (((0,), (0,)), ((), ()))


def dot32(a, b, dims):
    return lax.dot_general(a, b, dims, precision=EXACT, preferred_element_type=F32)


def dot16(a, b, dims):
    return lax.dot_general(a, b, dims, preferred_element_type=F32)


def split2(x):
    high = x.astype(BF16)
    low = (x - high.astype(F32)).astype(BF16)
    return high, low


def split3(x):
    high = x.astype(BF16)
    rest = x - high.astype(F32)
    mid = rest.astype(BF16)
    low = (rest - mid.astype(F32)).astype(BF16)
    return high, mid, low


def planes_kernel(me_ref, core_ref, x_ref, out_ref):
    ib = x_ref.shape[1]
    rows = x_ref.shape[3]
    flat = out_ref.reshape(rows * ib, out_ref.shape[2])
    for i in range(ib):
        pair = jnp.concatenate([x_ref[0, i], x_ref[1, i]], axis=0)
        flat[pl.ds(i, rows, stride=ib), :] = pair.T


def planes_first(me, core, field):
    species, cells, points, planes = field.shape
    ib = 8
    blocks = cells // ib
    return pl.pallas_call(
        planes_kernel,
        grid=(species // 2, blocks),
        in_specs=[pl.BlockSpec(memory_space=pltpu.SMEM)] * 2
        + [pl.BlockSpec((2, ib, points, planes), lambda c, g: (c, g, 0, 0))],
        out_specs=pl.BlockSpec((planes, ib, 2 * points), lambda c, g: (0, c * blocks + g, 0)),
        out_shape=pltpu.VMEM((planes, cells * species // 2, 2 * points), F32),
        compiler_params=pltpu.CompilerParams(vmem_limit_bytes=52 * MIB),
        name="planes_first",
    )(me, core, field)


def lower_blocks(n):
    return [(r, c) for r in range(n) for c in range(r + 1)]


def store_lower(core_ref, keep_ref, send_ref, packed, main, cross):
    n = main.shape[0] // 128
    for b, (r, c) in enumerate(lower_blocks(n)):
        rs, cs = slice(128 * r, 128 * r + 128), slice(128 * c, 128 * c + 128)
        packed[128 * b : 128 * b + 128, :] = main[rs, cs] + cross[rs, cs] + cross[cs, rs].T
    half = keep_ref.shape[0]
    keep_ref[...] = packed[pl.ds(pl.multiple_of(core_ref[0] * half, half), half), :]
    send_ref[...] = packed[pl.ds(pl.multiple_of((1 - core_ref[0]) * half, half), half), :]


def accumulate(step, main, cross, above, below, mixed):
    @pl.when(step == 0)
    def _():
        main[:256, :256] = above
        main[256:, :] = below
        cross[...] = mixed

    @pl.when(step > 0)
    def _():
        main[:256, :256] += above
        main[256:, :] += below
        cross[...] += mixed


def gram_first_kernel(steps, core_ref, y_ref, keep_ref, send_ref, packed, main, cross):
    step = pl.program_id(0)
    size = main.shape[0]
    parts = [
        y_ref[:, n, tau, c].reshape(size, 128)
        for n in range(y_ref.shape[1])
        for tau in range(2)
        for c in range(2)
    ]
    high, low = split2(jnp.concatenate(parts, axis=1))
    mixed = dot16(high, low, NT)
    above = dot16(high[:256], high[:256], NT)
    below = dot16(high[256:], high, NT)
    accumulate(step, main, cross, above, below, mixed)

    @pl.when(step == steps - 1)
    def _():
        store_lower(core_ref, keep_ref, send_ref, packed, main, cross)


GRAM_POINTS = 2


def gram_first(core, y):
    wide, narrow, _, groups, cells, lanes = y.shape
    size = wide * cells
    count = size // 128
    rows = 128 * (count * (count + 1) // 2)
    steps = narrow // GRAM_POINTS
    return pl.pallas_call(
        functools.partial(gram_first_kernel, steps),
        grid=(steps,),
        in_specs=[
            pl.BlockSpec(memory_space=pltpu.SMEM),
            pl.BlockSpec(
                (wide, GRAM_POINTS, 2, groups, cells, lanes), lambda g: (0, g, 0, 0, 0, 0)
            ),
        ],
        out_specs=[pl.BlockSpec((rows // 2, 128), lambda g: (0, 0))] * 2,
        out_shape=[jax.ShapeDtypeStruct((rows // 2, 128), F32)] * 2,
        scratch_shapes=[
            pltpu.VMEM((rows, 128), F32),
            pltpu.VMEM((size, size), F32),
            pltpu.VMEM((size, size), F32),
        ],
        compiler_params=pltpu.CompilerParams(vmem_limit_bytes=50 * MIB),
        name="gram_first",
    )(core, y)


def paired(keep, send):
    return keep + lax.ppermute(send, "core", SWAP)


def summed_pieces(half, chips):
    pieces = half.reshape(chips, 1, half.shape[0] * 128 // chips)
    return jnp.sum(lax.all_to_all(pieces, CHIPS, 0, 0, tiled=True), axis=0)


def gathered_half(own, chips):
    copies = jnp.broadcast_to(own[None], (chips, *own.shape))
    return lax.all_to_all(copies, CHIPS, 0, 0, tiled=True).reshape(-1, 128)


def swapped(mine):
    return lax.ppermute(mine, "core", SWAP)


WINDOW, PANEL = 32, 16


def inverse_factor(gram):
    size = gram.shape[0]
    row = lax.broadcasted_iota(jnp.int32, (size, size), 0)
    col = lax.broadcasted_iota(jnp.int32, (size, size), 1)
    work = jnp.concatenate([gram, jnp.where(row == col, 1.0, 0.0).astype(F32)], axis=1)
    low = lax.broadcasted_iota(jnp.int32, (8, size), 0)
    blocks = WINDOW // 8

    def spread(x):
        return jnp.broadcast_to(x, (8, x.shape[1]))

    done, scales = [], []
    for base in range(0, size, WINDOW):
        rows = [work[8 * i : 8 * i + 8] for i in range(blocks)]
        inverses, pivots = [None] * blocks, [None] * blocks
        for first in range(0, WINDOW, PANEL):
            cols = {}
            for j in range(PANEL):
                c = base + first + j
                for i in range(first // 8, blocks):
                    cols[j, i] = jnp.broadcast_to(rows[i][:, c : c + 1], (8, size))
            for k in range(PANEL):
                here, at = (first + k) // 8, k % 8
                pivot = spread(cols[k, here][at : at + 1])
                inverse = 1.0 / pivot
                ratio = {i: cols[k, i] * inverse for i in range(here, blocks)}
                ratio[here] = jnp.where(low > at, ratio[here], 0.0)
                for j in range(k + 1, PANEL):
                    piece = spread(cols[j, here][at : at + 1])
                    for i in range(here, blocks):
                        cols[j, i] = cols[j, i] - ratio[i] * piece
                piece = spread(rows[here][at : at + 1])
                for i in range(here, blocks):
                    rows[i] = rows[i] - jnp.concatenate([ratio[i], ratio[i]], axis=1) * piece
                inverses[here] = jnp.where(low == at, inverse, inverses[here]) if at else inverse
                pivots[here] = jnp.where(low == at, pivot, pivots[here]) if at else pivot
        done += [r[:, size:] for r in rows]
        scales += pivots
        if base + WINDOW < size:
            left = [r[:, :size] * s for r, s in zip(rows, inverses)]
            lh, lm, ll = split3(jnp.concatenate(left, axis=0))
            rh, rm, rl = split3(jnp.concatenate(rows, axis=0))
            lhs = jnp.concatenate([lh, lh, lh, lm, lm, ll], axis=0)
            rhs = jnp.concatenate([rh, rm, rl, rh, rm, rh], axis=0)
            work = work[WINDOW:] - dot16(lhs, rhs, TN)[base + WINDOW :]
    return jnp.concatenate([d * (1.0 / jnp.sqrt(p)) for d, p in zip(done, scales)], axis=0)


def orthonormal_rows(rows):
    rank = rows.shape[0]
    h, m, l = split3(rows)
    stack = jnp.concatenate([h, m, l], axis=0)
    d = dot16(stack, stack, NT)
    a, b = slice(0, rank), slice(rank, 2 * rank)
    c = slice(2 * rank, 3 * rank)
    gram = d[a, a] + (d[a, b] + d[b, a]) + (d[b, b] + (d[a, c] + d[c, a]))
    th, tm, tl = split3(inverse_factor(gram))
    return dot16(
        jnp.concatenate([th, th, th, tm, tm, tl], axis=1),
        jnp.concatenate([h, m, l, h, m, h], axis=0),
        NN,
    )


def start_kernel(start_ref, out_ref):
    out_ref[...] = orthonormal_rows(start_ref[...].T)


def start_rows(start):
    return pl.pallas_call(
        start_kernel,
        out_shape=jax.ShapeDtypeStruct(start.shape[::-1], F32),
        compiler_params=pltpu.CompilerParams(vmem_limit_bytes=8 * MIB),
        name="start_rows",
    )(start)


def basis_kernel(core_ref, mine_ref, other_ref, start_ref, rows_ref, packed, gram):
    half = mine_ref.shape[0]
    packed[pl.ds(pl.multiple_of(core_ref[0] * half, half), half), :] = mine_ref[...]
    packed[pl.ds(pl.multiple_of((1 - core_ref[0]) * half, half), half), :] = other_ref[...]
    n = gram.shape[0] // 128
    for b, (r, c) in enumerate(lower_blocks(n)):
        rs, cs = slice(128 * r, 128 * r + 128), slice(128 * c, 128 * c + 128)
        block = packed[128 * b : 128 * b + 128, :]
        gram[rs, cs] = block
        if r != c:
            gram[cs, rs] = block.T

    def sweep(_, rows):
        return orthonormal_rows(dot32(rows, gram[...], NN))

    rows_ref[...] = lax.fori_loop(0, ITERS, sweep, start_ref[...])


def basis_rows(core, mine, other, start):
    rank, size = start.shape
    whole = pl.BlockSpec(memory_space=pltpu.VMEM)
    return pl.pallas_call(
        basis_kernel,
        in_specs=[pl.BlockSpec(memory_space=pltpu.SMEM), whole, whole, whole],
        out_shape=jax.ShapeDtypeStruct((rank, size), F32),
        scratch_shapes=[
            pltpu.VMEM((2 * mine.shape[0], 128), F32),
            pltpu.VMEM((size, size), F32),
        ],
        compiler_params=pltpu.CompilerParams(vmem_limit_bytes=16 * MIB),
        name="basis_rows",
    )(core, mine, other, start)


def flip_kernel(rows_ref, out_ref):
    out_ref[...] = rows_ref[...].T


def flipped(rows):
    return pl.pallas_call(
        flip_kernel,
        out_shape=jax.ShapeDtypeStruct(rows.shape[::-1], F32),
        compiler_params=pltpu.CompilerParams(vmem_limit_bytes=4 * MIB),
        name="flipped",
    )(rows)


def reduce_kernel(me_ref, core_ref, rows_ref, y_ref, *refs):
    *out_refs, keep_ref, send_ref, packed, reduced, main, cross = refs
    step = pl.program_id(0)
    rank, size = rows_ref.shape
    narrow = len(out_refs)
    per = rank // narrow
    bh, bl = split2(rows_ref[...])
    both = jnp.concatenate([bh, bl], axis=0)
    lane = lax.broadcasted_iota(jnp.int32, (rank, 128), 1)
    for m in range(narrow // 2):
        parts = [y_ref[:, 2 * m + h, 0, 0].reshape(size, 128) for h in range(2)]
        yh, yl = split2(jnp.concatenate(parts, axis=1))
        wide = dot16(both, yh, NN)
        got = wide[:rank] + (wide[rank:] + dot16(bh, yl, NN))
        a, b = got[:, :128], got[:, 128:]
        lanes = slice(128 * m, 128 * m + 128)
        reduced[:rank, lanes] = jnp.where(lane < 64, a, pltpu.roll(b, 64, 1))
        reduced[rank:, lanes] = jnp.where(lane < 64, pltpu.roll(a, 64, 1), b)
    for j, out_ref in enumerate(out_refs):
        owner = lax.rem(me_ref[0] + j, narrow)
        for s in range(2):
            start = pl.multiple_of(rank * s + owner * per, per)
            out_ref[0, s] = reduced[pl.ds(start, per), :]
    high, low = split2(reduced[...])
    mixed = dot16(high, low, TN)
    above = dot16(high[:, :256], high[:, :256], TN)
    below = dot16(high[:, 256:], high, TN)
    accumulate(step, main, cross, above, below, mixed)

    @pl.when(step == 3)
    def _():
        store_lower(core_ref, keep_ref, send_ref, packed, main, cross)


def reduce_first(me, core, rows, y):
    wide, narrow, _, groups, cells, lanes = y.shape
    rank, size = rows.shape
    points = narrow * 64
    count = points // 128
    packed = 128 * (count * (count + 1) // 2)
    per = rank // narrow
    *blocks, keep, send = pl.pallas_call(
        reduce_kernel,
        grid=(2 * groups,),
        in_specs=[
            pl.BlockSpec(memory_space=pltpu.SMEM),
            pl.BlockSpec(memory_space=pltpu.SMEM),
            pl.BlockSpec((rank, size), lambda g: (0, 0)),
            pl.BlockSpec((wide, narrow, 1, 1, cells, lanes), lambda g: (0, 0, g % 2, g // 2, 0, 0)),
        ],
        out_specs=[pl.BlockSpec((1, 2, per, points), lambda g: (g, 0, 0, 0))] * narrow
        + [pl.BlockSpec((packed // 2, 128), lambda g: (0, 0))] * 2,
        out_shape=[jax.ShapeDtypeStruct((2 * groups, 2, per, points), F32)] * narrow
        + [jax.ShapeDtypeStruct((packed // 2, 128), F32)] * 2,
        scratch_shapes=[
            pltpu.VMEM((packed, 128), F32),
            pltpu.VMEM((2 * rank, points), F32),
            pltpu.VMEM((points, points), F32),
            pltpu.VMEM((points, points), F32),
        ],
        compiler_params=pltpu.CompilerParams(vmem_limit_bytes=48 * MIB),
        name="reduce_first",
    )(me, core, rows, y)
    return blocks, keep, send


def core_kernel(me_ref, rows_ref, *refs):
    *block_refs, out_ref = refs
    narrow = len(block_refs)
    taus, lows, per, points = block_refs[0].shape
    rank = rows_ref.shape[0]
    count = taus * lows * per
    bh, bl = split2(rows_ref[...])
    both = jnp.concatenate([bh, bl], axis=0)
    rows = jnp.concatenate([r[...].reshape(count, points) for r in block_refs], axis=0)
    rh, rl = split2(rows)
    wide = dot16(rh, both, NT)
    got = wide[:, :rank] + (wide[:, rank:] + dot16(rl, bh, NT))
    for j in range(narrow):
        source = lax.rem(me_ref[0] + (narrow - j), narrow)
        block = got[count * j : count * (j + 1)].reshape(taus, lows, per, rank)
        for tau in range(taus):
            out_ref[taus * source + tau] = block[tau]


def core_blocks(me, rows, blocks):
    rank, points = rows.shape
    narrow = len(blocks)
    steps, lows, per, _ = blocks[0].shape
    groups = steps // 2
    return pl.pallas_call(
        core_kernel,
        grid=(groups,),
        in_specs=[
            pl.BlockSpec(memory_space=pltpu.SMEM),
            pl.BlockSpec((rank, points), lambda g: (0, 0)),
        ]
        + [pl.BlockSpec((2, lows, per, points), lambda g: (g, 0, 0, 0))] * narrow,
        out_specs=pl.BlockSpec((2 * narrow, lows, per, rank), lambda g: (0, g, 0, 0)),
        out_shape=jax.ShapeDtypeStruct((2 * narrow, groups * lows, per, rank), F32),
        compiler_params=pltpu.CompilerParams(vmem_limit_bytes=12 * MIB),
        name="core_blocks",
    )(me, rows, *blocks)


def whole(field, start_first, start_second):
    narrow = lax.axis_size("narrow")
    wide = lax.axis_size("board") * lax.axis_size("core")
    chips = lax.axis_size("board") * narrow
    me = lax.axis_index("narrow").astype(jnp.int32).reshape(1)
    core = lax.axis_index("core").astype(jnp.int32).reshape(1)
    planes = lax.all_to_all(planes_first(me, core, field), ALL, 0, 0, tiled=True)
    y = planes.reshape(wide, narrow, 2, field.shape[0] // 2, field.shape[1], planes.shape[2])
    rows_first = start_rows(start_first)
    rows_second = start_rows(start_second)
    half = paired(*gram_first(core, y))
    own = summed_pieces(half, chips)
    mine = gathered_half(own, chips)
    rows_first = basis_rows(core, mine, swapped(mine), rows_first)
    blocks, keep, send = reduce_first(me, core, rows_first, y)
    half = paired(keep, send)
    own = summed_pieces(half, chips)
    moved = []
    for j in range(1, narrow):
        ring = [(n, (n + j) % narrow) for n in range(narrow)]
        moved.append(lax.ppermute(blocks[j], "narrow", ring))
    mine = gathered_half(own, chips)
    rows_second = basis_rows(core, mine, swapped(mine), rows_second)
    basis_first = flipped(rows_first)
    basis_second = flipped(rows_second)
    return (core_blocks(me, rows_second, [blocks[0]] + moved), basis_first, basis_second)


def solution(mesh):
    wide, narrow = mesh.devices.shape
    finer = Mesh(mesh.devices.reshape(wide // 2, 2, narrow), ALL)
    first = ("board", "core")
    return jax.shard_map(
        whole,
        mesh=finer,
        in_specs=(P(None, first, "narrow", None), P(), P()),
        out_specs=(P(first, None, "narrow", None), P(), P()),
        check_vma=False,
    )
```

```python
import functools
import jax
import jax.numpy as jnp
from jax import lax
from jax.experimental import pallas as pl
from jax.experimental.pallas import tpu as pltpu
from jax.sharding import Mesh, PartitionSpec as P

ITERS = 3
F32 = jnp.float32
BF16 = jnp.bfloat16
EXACT = lax.Precision.HIGHEST
ALL = ("board", "core", "narrow")
CHIPS = ("board", "narrow")
SWAP = [(0, 1), (1, 0)]
MIB = 1024 * 1024

NN = (((1,), (0,)), ((), ()))
NT = (((1,), (1,)), ((), ()))
TN = (((0,), (0,)), ((), ()))


def dot32(a, b, dims):
    return lax.dot_general(a, b, dims, precision=EXACT, preferred_element_type=F32)


def dot16(a, b, dims):
    return lax.dot_general(a, b, dims, preferred_element_type=F32)


def split2(x):
    high = x.astype(BF16)
    low = (x - high.astype(F32)).astype(BF16)
    return high, low


def split3(x):
    high = x.astype(BF16)
    rest = x - high.astype(F32)
    mid = rest.astype(BF16)
    low = (rest - mid.astype(F32)).astype(BF16)
    return high, mid, low


def planes_kernel(me_ref, core_ref, x_ref, out_ref):
    ib = x_ref.shape[1]
    rows = x_ref.shape[3]
    flat = out_ref.reshape(rows * ib, out_ref.shape[2])
    for i in range(ib):
        pair = jnp.concatenate([x_ref[0, i], x_ref[1, i]], axis=0)
        flat[pl.ds(i, rows, stride=ib), :] = pair.T


def planes_first(me, core, field):
    species, cells, points, planes = field.shape
    ib = 8
    blocks = cells // ib
    return pl.pallas_call(
        planes_kernel,
        grid=(species // 2, blocks),
        in_specs=[pl.BlockSpec(memory_space=pltpu.SMEM)] * 2
        + [pl.BlockSpec((2, ib, points, planes), lambda c, g: (c, g, 0, 0))],
        out_specs=pl.BlockSpec((planes, ib, 2 * points), lambda c, g: (0, c * blocks + g, 0)),
        out_shape=pltpu.VMEM((planes, cells * species // 2, 2 * points), F32),
        compiler_params=pltpu.CompilerParams(vmem_limit_bytes=52 * MIB),
        name="planes_first",
    )(me, core, field)


def lower_blocks(n):
    return [(r, c) for r in range(n) for c in range(r + 1)]


def store_lower(core_ref, keep_ref, send_ref, packed, main, cross):
    n = main.shape[0] // 128
    for b, (r, c) in enumerate(lower_blocks(n)):
        rs, cs = slice(128 * r, 128 * r + 128), slice(128 * c, 128 * c + 128)
        packed[128 * b : 128 * b + 128, :] = main[rs, cs] + cross[rs, cs] + cross[cs, rs].T
    half = keep_ref.shape[0]
    keep_ref[...] = packed[pl.ds(pl.multiple_of(core_ref[0] * half, half), half), :]
    send_ref[...] = packed[pl.ds(pl.multiple_of((1 - core_ref[0]) * half, half), half), :]


def accumulate(step, main, cross, above, below, mixed):
    @pl.when(step == 0)
    def _():
        main[:256, :256] = above
        main[256:, :] = below
        cross[...] = mixed

    @pl.when(step > 0)
    def _():
        main[:256, :256] += above
        main[256:, :] += below
        cross[...] += mixed


def gram_first_kernel(steps, core_ref, y_ref, keep_ref, send_ref, packed, main, cross):
    step = pl.program_id(0)
    size = main.shape[0]
    parts = [
        y_ref[:, n, tau, c].reshape(size, 128)
        for n in range(y_ref.shape[1])
        for tau in range(2)
        for c in range(2)
    ]
    high, low = split2(jnp.concatenate(parts, axis=1))
    mixed = dot16(high, low, NT)
    above = dot16(high[:256], high[:256], NT)
    below = dot16(high[256:], high, NT)
    accumulate(step, main, cross, above, below, mixed)

    @pl.when(step == steps - 1)
    def _():
        store_lower(core_ref, keep_ref, send_ref, packed, main, cross)


GRAM_POINTS = 2


def gram_first(core, y):
    wide, narrow, _, groups, cells, lanes = y.shape
    size = wide * cells
    count = size // 128
    rows = 128 * (count * (count + 1) // 2)
    steps = narrow // GRAM_POINTS
    return pl.pallas_call(
        functools.partial(gram_first_kernel, steps),
        grid=(steps,),
        in_specs=[
            pl.BlockSpec(memory_space=pltpu.SMEM),
            pl.BlockSpec(
                (wide, GRAM_POINTS, 2, groups, cells, lanes), lambda g: (0, g, 0, 0, 0, 0)
            ),
        ],
        out_specs=[pl.BlockSpec((rows // 2, 128), lambda g: (0, 0))] * 2,
        out_shape=[jax.ShapeDtypeStruct((rows // 2, 128), F32)] * 2,
        scratch_shapes=[
            pltpu.VMEM((rows, 128), F32),
            pltpu.VMEM((size, size), F32),
            pltpu.VMEM((size, size), F32),
        ],
        compiler_params=pltpu.CompilerParams(vmem_limit_bytes=50 * MIB),
        name="gram_first",
    )(core, y)


def paired(keep, send):
    return keep + lax.ppermute(send, "core", SWAP)


def summed_pieces(half, chips):
    pieces = half.reshape(chips, 1, half.shape[0] * 128 // chips)
    return jnp.sum(lax.all_to_all(pieces, CHIPS, 0, 0, tiled=True), axis=0)


def gathered_half(own, chips):
    copies = jnp.broadcast_to(own[None], (chips, *own.shape))
    return lax.all_to_all(copies, CHIPS, 0, 0, tiled=True).reshape(-1, 128)


def swapped(mine):
    return lax.ppermute(mine, "core", SWAP)


WINDOW, PANEL = 32, 16


def inverse_factor(gram):
    size = gram.shape[0]
    row = lax.broadcasted_iota(jnp.int32, (size, size), 0)
    col = lax.broadcasted_iota(jnp.int32, (size, size), 1)
    work = jnp.concatenate([gram, jnp.where(row == col, 1.0, 0.0).astype(F32)], axis=1)
    low = lax.broadcasted_iota(jnp.int32, (8, size), 0)
    blocks = WINDOW // 8

    def spread(x):
        return jnp.broadcast_to(x, (8, x.shape[1]))

    done, scales = [], []
    for base in range(0, size, WINDOW):
        rows = [work[8 * i : 8 * i + 8] for i in range(blocks)]
        inverses, pivots = [None] * blocks, [None] * blocks
        for first in range(0, WINDOW, PANEL):
            cols = {}
            for j in range(PANEL):
                c = base + first + j
                for i in range(first // 8, blocks):
                    cols[j, i] = jnp.broadcast_to(rows[i][:, c : c + 1], (8, size))
            for k in range(PANEL):
                here, at = (first + k) // 8, k % 8
                pivot = spread(cols[k, here][at : at + 1])
                inverse = 1.0 / pivot
                ratio = {i: cols[k, i] * inverse for i in range(here, blocks)}
                ratio[here] = jnp.where(low > at, ratio[here], 0.0)
                for j in range(k + 1, PANEL):
                    piece = spread(cols[j, here][at : at + 1])
                    for i in range(here, blocks):
                        cols[j, i] = cols[j, i] - ratio[i] * piece
                piece = spread(rows[here][at : at + 1])
                for i in range(here, blocks):
                    rows[i] = rows[i] - jnp.concatenate([ratio[i], ratio[i]], axis=1) * piece
                inverses[here] = jnp.where(low == at, inverse, inverses[here]) if at else inverse
                pivots[here] = jnp.where(low == at, pivot, pivots[here]) if at else pivot
        done += [r[:, size:] for r in rows]
        scales += pivots
        if base + WINDOW < size:
            left = [r[:, :size] * s for r, s in zip(rows, inverses)]
            lh, lm, ll = split3(jnp.concatenate(left, axis=0))
            rh, rm, rl = split3(jnp.concatenate(rows, axis=0))
            lhs = jnp.concatenate([lh, lh, lh, lm, lm, ll], axis=0)
            rhs = jnp.concatenate([rh, rm, rl, rh, rm, rh], axis=0)
            work = work[WINDOW:] - dot16(lhs, rhs, TN)[base + WINDOW :]
    return jnp.concatenate([d * (1.0 / jnp.sqrt(p)) for d, p in zip(done, scales)], axis=0)


def orthonormal_rows(rows):
    rank = rows.shape[0]
    h, m, l = split3(rows)
    stack = jnp.concatenate([h, m, l], axis=0)
    d = dot16(stack, stack, NT)
    a, b = slice(0, rank), slice(rank, 2 * rank)
    c = slice(2 * rank, 3 * rank)
    gram = d[a, a] + (d[a, b] + d[b, a]) + (d[b, b] + (d[a, c] + d[c, a]))
    th, tm, tl = split3(inverse_factor(gram))
    return dot16(
        jnp.concatenate([th, th, th, tm, tm, tl], axis=1),
        jnp.concatenate([h, m, l, h, m, h], axis=0),
        NN,
    )


def start_kernel(start_ref, out_ref):
    out_ref[...] = orthonormal_rows(start_ref[...].T)


def start_rows(start):
    return pl.pallas_call(
        start_kernel,
        out_shape=jax.ShapeDtypeStruct(start.shape[::-1], F32),
        compiler_params=pltpu.CompilerParams(vmem_limit_bytes=8 * MIB),
        name="start_rows",
    )(start)


def basis_kernel(core_ref, mine_ref, other_ref, start_ref, rows_ref, packed, gram):
    half = mine_ref.shape[0]
    packed[pl.ds(pl.multiple_of(core_ref[0] * half, half), half), :] = mine_ref[...]
    packed[pl.ds(pl.multiple_of((1 - core_ref[0]) * half, half), half), :] = other_ref[...]
    n = gram.shape[0] // 128
    for b, (r, c) in enumerate(lower_blocks(n)):
        rs, cs = slice(128 * r, 128 * r + 128), slice(128 * c, 128 * c + 128)
        block = packed[128 * b : 128 * b + 128, :]
        gram[rs, cs] = block
        if r != c:
            gram[cs, rs] = block.T

    def sweep(_, rows):
        return orthonormal_rows(dot32(rows, gram[...], NN))

    rows_ref[...] = lax.fori_loop(0, ITERS, sweep, start_ref[...])


def basis_rows(core, mine, other, start):
    rank, size = start.shape
    whole = pl.BlockSpec(memory_space=pltpu.VMEM)
    return pl.pallas_call(
        basis_kernel,
        in_specs=[pl.BlockSpec(memory_space=pltpu.SMEM), whole, whole, whole],
        out_shape=jax.ShapeDtypeStruct((rank, size), F32),
        scratch_shapes=[
            pltpu.VMEM((2 * mine.shape[0], 128), F32),
            pltpu.VMEM((size, size), F32),
        ],
        compiler_params=pltpu.CompilerParams(vmem_limit_bytes=16 * MIB),
        name="basis_rows",
    )(core, mine, other, start)


def flip_kernel(rows_ref, out_ref):
    out_ref[...] = rows_ref[...].T


def flipped(rows):
    return pl.pallas_call(
        flip_kernel,
        out_shape=jax.ShapeDtypeStruct(rows.shape[::-1], F32),
        compiler_params=pltpu.CompilerParams(vmem_limit_bytes=4 * MIB),
        name="flipped",
    )(rows)


def reduce_kernel(me_ref, core_ref, rows_ref, y_ref, *refs):
    *out_refs, keep_ref, send_ref, packed, reduced, main, cross = refs
    step = pl.program_id(0)
    rank, size = rows_ref.shape
    narrow = len(out_refs)
    per = rank // narrow
    bh, bl = split2(rows_ref[...])
    both = jnp.concatenate([bh, bl], axis=0)
    lane = lax.broadcasted_iota(jnp.int32, (rank, 128), 1)
    for m in range(narrow // 2):
        parts = [y_ref[:, 2 * m + h, 0, 0].reshape(size, 128) for h in range(2)]
        yh, yl = split2(jnp.concatenate(parts, axis=1))
        wide = dot16(both, yh, NN)
        got = wide[:rank] + (wide[rank:] + dot16(bh, yl, NN))
        a, b = got[:, :128], got[:, 128:]
        lanes = slice(128 * m, 128 * m + 128)
        reduced[:rank, lanes] = jnp.where(lane < 64, a, pltpu.roll(b, 64, 1))
        reduced[rank:, lanes] = jnp.where(lane < 64, pltpu.roll(a, 64, 1), b)
    for j, out_ref in enumerate(out_refs):
        owner = lax.rem(me_ref[0] + j, narrow)
        for s in range(2):
            start = pl.multiple_of(rank * s + owner * per, per)
            out_ref[0, s] = reduced[pl.ds(start, per), :]
    high, low = split2(reduced[...])
    mixed = dot16(high, low, TN)
    above = dot16(high[:, :256], high[:, :256], TN)
    below = dot16(high[:, 256:], high, TN)
    accumulate(step, main, cross, above, below, mixed)

    @pl.when(step == 3)
    def _():
        store_lower(core_ref, keep_ref, send_ref, packed, main, cross)


def reduce_first(me, core, rows, y):
    wide, narrow, _, groups, cells, lanes = y.shape
    rank, size = rows.shape
    points = narrow * 64
    count = points // 128
    packed = 128 * (count * (count + 1) // 2)
    per = rank // narrow
    *blocks, keep, send = pl.pallas_call(
        reduce_kernel,
        grid=(2 * groups,),
        in_specs=[
            pl.BlockSpec(memory_space=pltpu.SMEM),
            pl.BlockSpec(memory_space=pltpu.SMEM),
            pl.BlockSpec((rank, size), lambda g: (0, 0)),
            pl.BlockSpec((wide, narrow, 1, 1, cells, lanes), lambda g: (0, 0, g % 2, g // 2, 0, 0)),
        ],
        out_specs=[pl.BlockSpec((1, 2, per, points), lambda g: (g, 0, 0, 0))] * narrow
        + [pl.BlockSpec((packed // 2, 128), lambda g: (0, 0))] * 2,
        out_shape=[jax.ShapeDtypeStruct((2 * groups, 2, per, points), F32)] * narrow
        + [jax.ShapeDtypeStruct((packed // 2, 128), F32)] * 2,
        scratch_shapes=[
            pltpu.VMEM((packed, 128), F32),
            pltpu.VMEM((2 * rank, points), F32),
            pltpu.VMEM((points, points), F32),
            pltpu.VMEM((points, points), F32),
        ],
        compiler_params=pltpu.CompilerParams(vmem_limit_bytes=48 * MIB),
        name="reduce_first",
    )(me, core, rows, y)
    return blocks, keep, send


def core_kernel(me_ref, rows_ref, *refs):
    *block_refs, out_ref, basis_ref = refs

    @pl.when(pl.program_id(0) == 0)
    def _():
        basis_ref[...] = rows_ref[...].T

    narrow = len(block_refs)
    taus, lows, per, points = block_refs[0].shape
    rank = rows_ref.shape[0]
    count = taus * lows * per
    bh, bl = split2(rows_ref[...])
    both = jnp.concatenate([bh, bl], axis=0)
    rows = jnp.concatenate([r[...].reshape(count, points) for r in block_refs], axis=0)
    rh, rl = split2(rows)
    wide = dot16(rh, both, NT)
    got = wide[:, :rank] + (wide[:, rank:] + dot16(rl, bh, NT))
    for j in range(narrow):
        source = lax.rem(me_ref[0] + (narrow - j), narrow)
        block = got[count * j : count * (j + 1)].reshape(taus, lows, per, rank)
        for tau in range(taus):
            out_ref[taus * source + tau] = block[tau]


def core_blocks(me, rows, blocks):
    rank, points = rows.shape
    narrow = len(blocks)
    steps, lows, per, _ = blocks[0].shape
    groups = steps // 2
    return pl.pallas_call(
        core_kernel,
        grid=(groups,),
        in_specs=[
            pl.BlockSpec(memory_space=pltpu.SMEM),
            pl.BlockSpec((rank, points), lambda g: (0, 0)),
        ]
        + [pl.BlockSpec((2, lows, per, points), lambda g: (g, 0, 0, 0))] * narrow,
        out_specs=(
            pl.BlockSpec((2 * narrow, lows, per, rank), lambda g: (0, g, 0, 0)),
            pl.BlockSpec((points, rank), lambda g: (0, 0)),
        ),
        out_shape=(
            jax.ShapeDtypeStruct((2 * narrow, groups * lows, per, rank), F32),
            jax.ShapeDtypeStruct((points, rank), F32),
        ),
        compiler_params=pltpu.CompilerParams(vmem_limit_bytes=12 * MIB),
        name="core_blocks",
    )(me, rows, *blocks)


def whole(field, start_first, start_second):
    narrow = lax.axis_size("narrow")
    wide = lax.axis_size("board") * lax.axis_size("core")
    chips = lax.axis_size("board") * narrow
    me = lax.axis_index("narrow").astype(jnp.int32).reshape(1)
    core = lax.axis_index("core").astype(jnp.int32).reshape(1)
    planes = lax.all_to_all(planes_first(me, core, field), ALL, 0, 0, tiled=True)
    y = planes.reshape(wide, narrow, 2, field.shape[0] // 2, field.shape[1], planes.shape[2])
    rows_first = start_rows(start_first)
    rows_second = start_rows(start_second)
    half = paired(*gram_first(core, y))
    own = summed_pieces(half, chips)
    mine = gathered_half(own, chips)
    rows_first = basis_rows(core, mine, swapped(mine), rows_first)
    blocks, keep, send = reduce_first(me, core, rows_first, y)
    half = paired(keep, send)
    own = summed_pieces(half, chips)
    moved = []
    for j in range(1, narrow):
        ring = [(n, (n + j) % narrow) for n in range(narrow)]
        moved.append(lax.ppermute(blocks[j], "narrow", ring))
    mine = gathered_half(own, chips)
    rows_second = basis_rows(core, mine, swapped(mine), rows_second)
    basis_first = flipped(rows_first)
    tensor, basis_second = core_blocks(me, rows_second, [blocks[0]] + moved)
    return (tensor, basis_first, basis_second)


def solution(mesh):
    wide, narrow = mesh.devices.shape
    finer = Mesh(mesh.devices.reshape(wide // 2, 2, narrow), ALL)
    first = ("board", "core")
    return jax.shard_map(
        whole,
        mesh=finer,
        in_specs=(P(None, first, "narrow", None), P(), P()),
        out_specs=(P(first, None, "narrow", None), P(), P()),
        check_vma=False,
    )
```

```python
import functools
import jax
import jax.numpy as jnp
from jax import lax
from jax.experimental import pallas as pl
from jax.experimental.pallas import tpu as pltpu
from jax.sharding import Mesh, PartitionSpec as P

ITERS = 3
F32 = jnp.float32
BF16 = jnp.bfloat16
EXACT = lax.Precision.HIGHEST
ALL = ("board", "core", "narrow")
CHIPS = ("board", "narrow")
SWAP = [(0, 1), (1, 0)]
MIB = 1024 * 1024

NN = (((1,), (0,)), ((), ()))
NT = (((1,), (1,)), ((), ()))
TN = (((0,), (0,)), ((), ()))


def dot32(a, b, dims):
    return lax.dot_general(a, b, dims, precision=EXACT, preferred_element_type=F32)


def dot16(a, b, dims):
    return lax.dot_general(a, b, dims, preferred_element_type=F32)


def split2(x):
    high = x.astype(BF16)
    low = (x - high.astype(F32)).astype(BF16)
    return high, low


def split3(x):
    high = x.astype(BF16)
    rest = x - high.astype(F32)
    mid = rest.astype(BF16)
    low = (rest - mid.astype(F32)).astype(BF16)
    return high, mid, low


def planes_kernel(me_ref, core_ref, x_ref, out_ref):
    ib = x_ref.shape[1]
    rows = x_ref.shape[3]
    every = out_ref.shape[1]
    flat = out_ref.reshape(rows * every, out_ref.shape[2])
    base = (pl.program_id(0) * pl.num_programs(1) + pl.program_id(1)) * ib
    for i in range(ib):
        pair = jnp.concatenate([x_ref[0, i], x_ref[1, i]], axis=0)
        flat[pl.ds(base + i, rows, stride=every), :] = pair.T


def planes_first(me, core, field):
    species, cells, points, planes = field.shape
    ib = 8
    blocks = cells // ib
    return pl.pallas_call(
        planes_kernel,
        grid=(species // 2, blocks),
        in_specs=[pl.BlockSpec(memory_space=pltpu.SMEM)] * 2
        + [pl.BlockSpec((2, ib, points, planes), lambda c, g: (c, g, 0, 0))],
        out_specs=pl.BlockSpec(memory_space=pltpu.VMEM),
        out_shape=pltpu.VMEM((planes, cells * species // 2, 2 * points), F32),
        compiler_params=pltpu.CompilerParams(vmem_limit_bytes=52 * MIB),
        name="planes_first",
    )(me, core, field)


def lower_blocks(n):
    return [(r, c) for r in range(n) for c in range(r + 1)]


def store_lower(core_ref, keep_ref, send_ref, packed, main, cross):
    n = main.shape[0] // 128
    for b, (r, c) in enumerate(lower_blocks(n)):
        rs, cs = slice(128 * r, 128 * r + 128), slice(128 * c, 128 * c + 128)
        packed[128 * b : 128 * b + 128, :] = main[rs, cs] + cross[rs, cs] + cross[cs, rs].T
    half = keep_ref.shape[0]
    keep_ref[...] = packed[pl.ds(pl.multiple_of(core_ref[0] * half, half), half), :]
    send_ref[...] = packed[pl.ds(pl.multiple_of((1 - core_ref[0]) * half, half), half), :]


def accumulate(step, main, cross, above, below, mixed):
    @pl.when(step == 0)
    def _():
        main[:256, :256] = above
        main[256:, :] = below
        cross[...] = mixed

    @pl.when(step > 0)
    def _():
        main[:256, :256] += above
        main[256:, :] += below
        cross[...] += mixed


def gram_first_kernel(steps, core_ref, y_ref, keep_ref, send_ref, packed, main, cross):
    step = pl.program_id(0)
    size = main.shape[0]
    parts = [
        y_ref[:, n, tau, c].reshape(size, 128)
        for n in range(y_ref.shape[1])
        for tau in range(2)
        for c in range(2)
    ]
    high, low = split2(jnp.concatenate(parts, axis=1))
    mixed = dot16(high, low, NT)
    above = dot16(high[:256], high[:256], NT)
    below = dot16(high[256:], high, NT)
    accumulate(step, main, cross, above, below, mixed)

    @pl.when(step == steps - 1)
    def _():
        store_lower(core_ref, keep_ref, send_ref, packed, main, cross)


GRAM_POINTS = 2


def gram_first(core, y):
    wide, narrow, _, groups, cells, lanes = y.shape
    size = wide * cells
    count = size // 128
    rows = 128 * (count * (count + 1) // 2)
    steps = narrow // GRAM_POINTS
    return pl.pallas_call(
        functools.partial(gram_first_kernel, steps),
        grid=(steps,),
        in_specs=[
            pl.BlockSpec(memory_space=pltpu.SMEM),
            pl.BlockSpec(
                (wide, GRAM_POINTS, 2, groups, cells, lanes), lambda g: (0, g, 0, 0, 0, 0)
            ),
        ],
        out_specs=[pl.BlockSpec((rows // 2, 128), lambda g: (0, 0))] * 2,
        out_shape=[jax.ShapeDtypeStruct((rows // 2, 128), F32)] * 2,
        scratch_shapes=[
            pltpu.VMEM((rows, 128), F32),
            pltpu.VMEM((size, size), F32),
            pltpu.VMEM((size, size), F32),
        ],
        compiler_params=pltpu.CompilerParams(vmem_limit_bytes=50 * MIB),
        name="gram_first",
    )(core, y)


def paired(keep, send):
    return keep + lax.ppermute(send, "core", SWAP)


def summed_pieces(half, chips):
    pieces = half.reshape(chips, 1, half.shape[0] * 128 // chips)
    return jnp.sum(lax.all_to_all(pieces, CHIPS, 0, 0, tiled=True), axis=0)


def gathered_half(own, chips):
    copies = jnp.broadcast_to(own[None], (chips, *own.shape))
    return lax.all_to_all(copies, CHIPS, 0, 0, tiled=True).reshape(-1, 128)


def swapped(mine):
    return lax.ppermute(mine, "core", SWAP)


WINDOW, PANEL = 32, 16


def inverse_factor(gram):
    size = gram.shape[0]
    row = lax.broadcasted_iota(jnp.int32, (size, size), 0)
    col = lax.broadcasted_iota(jnp.int32, (size, size), 1)
    work = jnp.concatenate([gram, jnp.where(row == col, 1.0, 0.0).astype(F32)], axis=1)
    low = lax.broadcasted_iota(jnp.int32, (8, size), 0)
    blocks = WINDOW // 8

    def spread(x):
        return jnp.broadcast_to(x, (8, x.shape[1]))

    done, scales = [], []
    for base in range(0, size, WINDOW):
        rows = [work[8 * i : 8 * i + 8] for i in range(blocks)]
        inverses, pivots = [None] * blocks, [None] * blocks
        for first in range(0, WINDOW, PANEL):
            cols = {}
            for j in range(PANEL):
                c = base + first + j
                for i in range(first // 8, blocks):
                    cols[j, i] = jnp.broadcast_to(rows[i][:, c : c + 1], (8, size))
            for k in range(PANEL):
                here, at = (first + k) // 8, k % 8
                pivot = spread(cols[k, here][at : at + 1])
                inverse = 1.0 / pivot
                ratio = {i: cols[k, i] * inverse for i in range(here, blocks)}
                ratio[here] = jnp.where(low > at, ratio[here], 0.0)
                for j in range(k + 1, PANEL):
                    piece = spread(cols[j, here][at : at + 1])
                    for i in range(here, blocks):
                        cols[j, i] = cols[j, i] - ratio[i] * piece
                piece = spread(rows[here][at : at + 1])
                for i in range(here, blocks):
                    rows[i] = rows[i] - jnp.concatenate([ratio[i], ratio[i]], axis=1) * piece
                inverses[here] = jnp.where(low == at, inverse, inverses[here]) if at else inverse
                pivots[here] = jnp.where(low == at, pivot, pivots[here]) if at else pivot
        done += [r[:, size:] for r in rows]
        scales += pivots
        if base + WINDOW < size:
            left = [r[:, :size] * s for r, s in zip(rows, inverses)]
            lh, lm, ll = split3(jnp.concatenate(left, axis=0))
            rh, rm, rl = split3(jnp.concatenate(rows, axis=0))
            lhs = jnp.concatenate([lh, lh, lh, lm, lm, ll], axis=0)
            rhs = jnp.concatenate([rh, rm, rl, rh, rm, rh], axis=0)
            work = work[WINDOW:] - dot16(lhs, rhs, TN)[base + WINDOW :]
    return jnp.concatenate([d * (1.0 / jnp.sqrt(p)) for d, p in zip(done, scales)], axis=0)


def orthonormal_rows(rows):
    rank = rows.shape[0]
    h, m, l = split3(rows)
    stack = jnp.concatenate([h, m, l], axis=0)
    d = dot16(stack, stack, NT)
    a, b = slice(0, rank), slice(rank, 2 * rank)
    c = slice(2 * rank, 3 * rank)
    gram = d[a, a] + (d[a, b] + d[b, a]) + (d[b, b] + (d[a, c] + d[c, a]))
    th, tm, tl = split3(inverse_factor(gram))
    return dot16(
        jnp.concatenate([th, th, th, tm, tm, tl], axis=1),
        jnp.concatenate([h, m, l, h, m, h], axis=0),
        NN,
    )


def start_kernel(start_ref, out_ref):
    out_ref[...] = orthonormal_rows(start_ref[...].T)


def start_rows(start):
    return pl.pallas_call(
        start_kernel,
        out_shape=jax.ShapeDtypeStruct(start.shape[::-1], F32),
        compiler_params=pltpu.CompilerParams(vmem_limit_bytes=8 * MIB),
        name="start_rows",
    )(start)


def basis_kernel(core_ref, mine_ref, other_ref, start_ref, rows_ref, packed, gram):
    half = mine_ref.shape[0]
    packed[pl.ds(pl.multiple_of(core_ref[0] * half, half), half), :] = mine_ref[...]
    packed[pl.ds(pl.multiple_of((1 - core_ref[0]) * half, half), half), :] = other_ref[...]
    n = gram.shape[0] // 128
    for b, (r, c) in enumerate(lower_blocks(n)):
        rs, cs = slice(128 * r, 128 * r + 128), slice(128 * c, 128 * c + 128)
        block = packed[128 * b : 128 * b + 128, :]
        gram[rs, cs] = block
        if r != c:
            gram[cs, rs] = block.T

    def sweep(_, rows):
        return orthonormal_rows(dot32(rows, gram[...], NN))

    rows_ref[...] = lax.fori_loop(0, ITERS, sweep, start_ref[...])


def basis_rows(core, mine, other, start):
    rank, size = start.shape
    whole = pl.BlockSpec(memory_space=pltpu.VMEM)
    return pl.pallas_call(
        basis_kernel,
        in_specs=[pl.BlockSpec(memory_space=pltpu.SMEM), whole, whole, whole],
        out_shape=jax.ShapeDtypeStruct((rank, size), F32),
        scratch_shapes=[
            pltpu.VMEM((2 * mine.shape[0], 128), F32),
            pltpu.VMEM((size, size), F32),
        ],
        compiler_params=pltpu.CompilerParams(vmem_limit_bytes=16 * MIB),
        name="basis_rows",
    )(core, mine, other, start)


def flip_kernel(rows_ref, out_ref):
    out_ref[...] = rows_ref[...].T


def flipped(rows):
    return pl.pallas_call(
        flip_kernel,
        out_shape=jax.ShapeDtypeStruct(rows.shape[::-1], F32),
        compiler_params=pltpu.CompilerParams(vmem_limit_bytes=4 * MIB),
        name="flipped",
    )(rows)


def reduce_kernel(me_ref, core_ref, rows_ref, y_ref, *refs):
    *out_refs, keep_ref, send_ref, packed, reduced, main, cross = refs
    step = pl.program_id(0)
    rank, size = rows_ref.shape
    narrow = len(out_refs)
    per = rank // narrow
    bh, bl = split2(rows_ref[...])
    both = jnp.concatenate([bh, bl], axis=0)
    lane = lax.broadcasted_iota(jnp.int32, (rank, 128), 1)
    for m in range(narrow // 2):
        parts = [y_ref[:, 2 * m + h, 0, 0].reshape(size, 128) for h in range(2)]
        yh, yl = split2(jnp.concatenate(parts, axis=1))
        wide = dot16(both, yh, NN)
        got = wide[:rank] + (wide[rank:] + dot16(bh, yl, NN))
        a, b = got[:, :128], got[:, 128:]
        lanes = slice(128 * m, 128 * m + 128)
        reduced[:rank, lanes] = jnp.where(lane < 64, a, pltpu.roll(b, 64, 1))
        reduced[rank:, lanes] = jnp.where(lane < 64, pltpu.roll(a, 64, 1), b)
    for j, out_ref in enumerate(out_refs):
        owner = lax.rem(me_ref[0] + j, narrow)
        for s in range(2):
            start = pl.multiple_of(rank * s + owner * per, per)
            out_ref[0, s] = reduced[pl.ds(start, per), :]
    high, low = split2(reduced[...])
    mixed = dot16(high, low, TN)
    above = dot16(high[:, :256], high[:, :256], TN)
    below = dot16(high[:, 256:], high, TN)
    accumulate(step, main, cross, above, below, mixed)

    @pl.when(step == 3)
    def _():
        store_lower(core_ref, keep_ref, send_ref, packed, main, cross)


def reduce_first(me, core, rows, y):
    wide, narrow, _, groups, cells, lanes = y.shape
    rank, size = rows.shape
    points = narrow * 64
    count = points // 128
    packed = 128 * (count * (count + 1) // 2)
    per = rank // narrow
    *blocks, keep, send = pl.pallas_call(
        reduce_kernel,
        grid=(2 * groups,),
        in_specs=[
            pl.BlockSpec(memory_space=pltpu.SMEM),
            pl.BlockSpec(memory_space=pltpu.SMEM),
            pl.BlockSpec((rank, size), lambda g: (0, 0)),
            pl.BlockSpec((wide, narrow, 1, 1, cells, lanes), lambda g: (0, 0, g % 2, g // 2, 0, 0)),
        ],
        out_specs=[pl.BlockSpec((1, 2, per, points), lambda g: (g, 0, 0, 0))] * narrow
        + [pl.BlockSpec((packed // 2, 128), lambda g: (0, 0))] * 2,
        out_shape=[jax.ShapeDtypeStruct((2 * groups, 2, per, points), F32)] * narrow
        + [jax.ShapeDtypeStruct((packed // 2, 128), F32)] * 2,
        scratch_shapes=[
            pltpu.VMEM((packed, 128), F32),
            pltpu.VMEM((2 * rank, points), F32),
            pltpu.VMEM((points, points), F32),
            pltpu.VMEM((points, points), F32),
        ],
        compiler_params=pltpu.CompilerParams(vmem_limit_bytes=48 * MIB),
        name="reduce_first",
    )(me, core, rows, y)
    return blocks, keep, send


def core_kernel(me_ref, rows_ref, *refs):
    *block_refs, out_ref, basis_ref = refs

    @pl.when(pl.program_id(0) == 0)
    def _():
        basis_ref[...] = rows_ref[...].T

    narrow = len(block_refs)
    taus, lows, per, points = block_refs[0].shape
    rank = rows_ref.shape[0]
    count = taus * lows * per
    bh, bl = split2(rows_ref[...])
    both = jnp.concatenate([bh, bl], axis=0)
    rows = jnp.concatenate([r[...].reshape(count, points) for r in block_refs], axis=0)
    rh, rl = split2(rows)
    wide = dot16(rh, both, NT)
    got = wide[:, :rank] + (wide[:, rank:] + dot16(rl, bh, NT))
    for j in range(narrow):
        source = lax.rem(me_ref[0] + (narrow - j), narrow)
        block = got[count * j : count * (j + 1)].reshape(taus, lows, per, rank)
        for tau in range(taus):
            out_ref[taus * source + tau] = block[tau]


def core_blocks(me, rows, blocks):
    rank, points = rows.shape
    narrow = len(blocks)
    steps, lows, per, _ = blocks[0].shape
    groups = steps // 2
    return pl.pallas_call(
        core_kernel,
        grid=(groups,),
        in_specs=[
            pl.BlockSpec(memory_space=pltpu.SMEM),
            pl.BlockSpec((rank, points), lambda g: (0, 0)),
        ]
        + [pl.BlockSpec((2, lows, per, points), lambda g: (g, 0, 0, 0))] * narrow,
        out_specs=(
            pl.BlockSpec((2 * narrow, lows, per, rank), lambda g: (0, g, 0, 0)),
            pl.BlockSpec((points, rank), lambda g: (0, 0)),
        ),
        out_shape=(
            jax.ShapeDtypeStruct((2 * narrow, groups * lows, per, rank), F32),
            jax.ShapeDtypeStruct((points, rank), F32),
        ),
        compiler_params=pltpu.CompilerParams(vmem_limit_bytes=12 * MIB),
        name="core_blocks",
    )(me, rows, *blocks)


def whole(field, start_first, start_second):
    narrow = lax.axis_size("narrow")
    wide = lax.axis_size("board") * lax.axis_size("core")
    chips = lax.axis_size("board") * narrow
    me = lax.axis_index("narrow").astype(jnp.int32).reshape(1)
    core = lax.axis_index("core").astype(jnp.int32).reshape(1)
    planes = lax.all_to_all(planes_first(me, core, field), ALL, 0, 0, tiled=True)
    y = planes.reshape(wide, narrow, 2, field.shape[0] // 2, field.shape[1], planes.shape[2])
    rows_first = start_rows(start_first)
    rows_second = start_rows(start_second)
    half = paired(*gram_first(core, y))
    own = summed_pieces(half, chips)
    mine = gathered_half(own, chips)
    rows_first = basis_rows(core, mine, swapped(mine), rows_first)
    blocks, keep, send = reduce_first(me, core, rows_first, y)
    half = paired(keep, send)
    own = summed_pieces(half, chips)
    moved = []
    for j in range(1, narrow):
        ring = [(n, (n + j) % narrow) for n in range(narrow)]
        moved.append(lax.ppermute(blocks[j], "narrow", ring))
    mine = gathered_half(own, chips)
    rows_second = basis_rows(core, mine, swapped(mine), rows_second)
    basis_first = flipped(rows_first)
    tensor, basis_second = core_blocks(me, rows_second, [blocks[0]] + moved)
    return (tensor, basis_first, basis_second)


def solution(mesh):
    wide, narrow = mesh.devices.shape
    finer = Mesh(mesh.devices.reshape(wide // 2, 2, narrow), ALL)
    first = ("board", "core")
    return jax.shard_map(
        whole,
        mesh=finer,
        in_specs=(P(None, first, "narrow", None), P(), P()),
        out_specs=(P(first, None, "narrow", None), P(), P()),
        check_vma=False,
    )
```
